32 devices in a mesh: win: 2 (over y), bl: 4 (over x, core), freq: 4 (over z).
Axes of the slice: x: 2, y: 2, z: 4, core: 2. Of those that a mesh axis runs over, the one named last changes fastest.
Arguments:
- vis: bfloat16 [64, 1536, 2, 512], P('bl', 'freq', None, 'win'), parts along dimension 3, may hold values from -6 to 6
- flags: int32 [64, 1536], P('bl', 'freq'), may hold values 0 or 1
- band: int32 [64], P('bl'), may hold values from 0 to 7
- group_id: int32 [64], P('bl'), may hold values from 0 to 7, as said below
Outputs:
- averaged: bfloat16 [8, 2, 512, 1536], P('bl', None, ('win', 'freq')), parts along dimension 2
The draws below stay inside these ranges and needn't reach their ends.
There are 2 independent parts, one for each index of `win`. The reference program is written for one: setup_inputs(seed, part) draws one part's arguments, and reference() takes and returns one part's arrays. A program takes and returns all parts, laid end to end along the dimension named above; an argument that names none is the same for every part. Nothing has to cross between parts.
Inputs may be any that keep to these rules, and one draw needn't show every extreme that they name: `group_id`: of each aligned block of 16 baselines (those of one index of bl), at most 8 belong to the groups of one owner; in every draw one owner receives exactly 8 from every block.
All inputs are finite; a program needn't handle non-finite values. No bound on the sum of `flags` on one device may be relied on, other than what follows from the above.
Results may differ from the reference program's by a relative error of at most 0.0071.
Values may be sent and summed in bfloat16 or wider, within the bound.
A program may use at most 64 MiB of HBM per device.

```python
import math
import jax
import jax.numpy as jnp
from jax import lax

CH = 1536
DELAYS = 128
NBAND = 8
TIME = 256
B_BL = 16
GPO = 2
CAP = 8
B = 64
NG = 8
N_BL = 4


def draw_group_id(key, part):
    key_busy, key_rest, key_order, key_local = jax.random.split(jax.random.fold_in(key, 17), 4)
    busiest = jax.random.randint(key_busy, (), 0, N_BL)
    others = jax.random.randint(key_rest, (N_BL, B_BL - CAP), 0, N_BL - 1)
    others = others + (others >= busiest).astype(jnp.int32)
    owner_of = jnp.concatenate([jnp.full((N_BL, CAP), 0, jnp.int32) + busiest, others], axis=1)
    order_keys = jax.random.split(key_order, N_BL)
    orders = jax.vmap(lambda sub_key: jax.random.permutation(sub_key, B_BL))(order_keys)
    owner_of = jnp.take_along_axis(owner_of, orders.astype(jnp.int32), axis=1)
    local_ids = jax.random.randint(key_local, (N_BL, B_BL), 0, GPO)
    return (owner_of * GPO + local_ids).reshape(N_BL * B_BL).astype(jnp.int32)


def plant(entries, rng, least, top_value):
    extent = entries.shape
    index_at = [jax.random.randint(jax.random.fold_in(rng, axis), (), 0, extent[axis]) for axis in range(len(extent))]
    entries = entries.at[tuple(index_at)].set(least)
    longest = extent.index(max(extent))
    index_at[longest] = (index_at[longest] + 1) % extent[longest]
    return entries.at[tuple(index_at)].set(top_value)


def block_levels(rng, dims, cuts, smallest, top_value):
    level, own = 1.0, jax.random.fold_in(rng, 6)
    for dim, shards_of in cuts:
        heights = jnp.exp(jax.random.uniform(jax.random.fold_in(own, dim), (shards_of,), jnp.float32, smallest / len(cuts), top_value / len(cuts)))
        level = level * jnp.repeat(heights, dims[dim] // shards_of).reshape([-1 if axis == dim else 1 for axis in range(len(dims))])
    return level


def scatter_about(key, dims, width, most, cuts=(), kind=jnp.bfloat16):
    array = width * jax.random.normal(key, dims, jnp.float32)
    if cuts:
        array = array * block_levels(key, dims, cuts, -0.22, 0.18)
    return jnp.clip(array, -most, most).astype(kind)


def setup_inputs(seed: int = 0, part: int = 0) -> dict:
    streams_of = jax.random.split(jax.random.key(seed), 5)
    part_keys = jax.random.split(jax.random.fold_in(streams_of[4], part), 5)
    vis = scatter_about(part_keys[0], (B, CH, 2, TIME), 1.0, 6.0, ((0, 4), (1, 4)))
    flags = plant((jax.random.randint(streams_of[1], (B, CH), 0, 8) < 1).astype(jnp.int32), jax.random.fold_in(streams_of[1], 1), 0, 1)
    band = plant(jax.random.randint(streams_of[2], (B,), 0, NBAND), jax.random.fold_in(streams_of[2], 1), 0, NBAND - 1).astype(jnp.int32)
    group_id = draw_group_id(jax.random.fold_in(streams_of[4], 71), part)
    return dict(vis=vis, flags=flags, band=band, group_id=group_id)


def fourier_tables(length):
    sample_index = jnp.arange(length, dtype=jnp.int32)
    phase_index = sample_index[:, None] * sample_index[None, :] % length
    angles = phase_index.astype(jnp.float32) * (2.0 * math.pi / length)
    cosine = jnp.cos(angles)
    sine_table = jnp.sin(angles)
    forward = jnp.concatenate([jnp.concatenate([cosine, -sine_table], 1), jnp.concatenate([sine_table, cosine], 1)], 0)
    inverse = jnp.concatenate([jnp.concatenate([cosine, sine_table], 1), jnp.concatenate([-sine_table, cosine], 1)], 0)
    return (forward.astype(jnp.bfloat16), inverse.astype(jnp.bfloat16))

def band_response(band, length, band_count):
    mode_index = jnp.arange(length, dtype=jnp.int32)
    signed_modes = (mode_index - length * (mode_index >= length // 2).astype(jnp.int32)).astype(jnp.float32)
    center = (band.astype(jnp.float32) - (band_count - 1) / 2.0) * (length / (4.0 * band_count))
    band_width = length / 32.0
    offset_ratio = (signed_modes[None, :] - center[:, None]) / band_width
    single = (0.15 + 0.85 / (1.0 + offset_ratio ** 4)) / length
    return jnp.concatenate([single, single], 1)

def make_basis(channels, modes):
    channel_index = jnp.arange(channels, dtype=jnp.int32)
    order_index = jnp.arange(modes, dtype=jnp.int32)
    phase_index = order_index[None, :] * (2 * channel_index[:, None] + 1) % (4 * channels)
    return jnp.cos(phase_index.astype(jnp.float32) * (math.pi / (2 * channels))).astype(jnp.bfloat16)

def reference(vis, flags, band, group_id):
    forward, inverse = fourier_tables(TIME)
    response = band_response(band, TIME, NBAND)

    def fringe_block(inputs):
        block, block_response = inputs
        flat_rows = block.reshape(B_BL * CH, 2 * TIME)
        spectra = jnp.dot(flat_rows.astype(jnp.float32), forward.astype(jnp.float32), preferred_element_type=jnp.float32).reshape(B_BL, CH, 2 * TIME)
        spectra = (spectra * block_response[:, None, :]).astype(jnp.bfloat16)
        result = jnp.dot(spectra.reshape(B_BL * CH, 2 * TIME).astype(jnp.float32), inverse.astype(jnp.float32), preferred_element_type=jnp.float32)
        return result.astype(jnp.bfloat16).reshape(B_BL, CH, 2, TIME)
    fringe = lax.map(fringe_block, (vis.reshape(N_BL, B_BL, CH, 2, TIME), response.reshape(N_BL, B_BL, 2 * TIME)))
    fringe = fringe.reshape(B, CH, 2, TIME)
    weight = 1.0 - flags.astype(jnp.float32)
    delay_basis = make_basis(CH, DELAYS)
    basis_wide = delay_basis.astype(jnp.float32)
    ridge_scale = CH / 64.0
    select = group_id[None, :] == jnp.arange(NG, dtype=jnp.int32)[:, None]
    counts = jnp.sum(select.astype(jnp.float32), 1)

    def clean_one(sums, inputs):
        column, weight_row, group_index = inputs
        normal = jnp.dot(basis_wide.T * weight_row[None, :], basis_wide, precision=lax.Precision.HIGHEST)
        normal = normal + ridge_scale * jnp.eye(DELAYS, dtype=jnp.float32)
        factor = jnp.linalg.cholesky(normal)
        masked = column * weight_row[:, None, None].astype(jnp.bfloat16)
        projected = jnp.einsum('crt,ck->krt', masked.astype(jnp.float32), basis_wide).reshape(DELAYS, 2 * TIME)
        half_solved = lax.linalg.triangular_solve(factor, projected, left_side=True, lower=True)
        coefficients = lax.linalg.triangular_solve(factor, half_solved, left_side=True, lower=True, transpose_a=True)
        coefficients = coefficients.reshape(DELAYS, 2, TIME)
        fitted = jnp.einsum('krt,ck->rtc', coefficients, basis_wide, precision=lax.Precision.HIGHEST)
        cleaned = (weight_row[None, None, :] * (jnp.transpose(column, (1, 2, 0)).astype(jnp.float32) - fitted)).astype(jnp.bfloat16)
        zero_index = jnp.zeros((), jnp.int32)
        start = (group_index.astype(jnp.int32), zero_index, zero_index, zero_index)
        current = lax.dynamic_slice(sums, start, (1, 2, TIME, CH))
        sums = lax.dynamic_update_slice(sums, current + cleaned.astype(jnp.float32)[None], start)
        return (sums, None)
    initial = jnp.zeros((NG, 2, TIME, CH), jnp.float32)
    group_sums, unused = lax.scan(clean_one, initial, (fringe, weight, group_id))
    return (group_sums / jnp.maximum(counts, 1.0)[:, None, None, None]).astype(jnp.bfloat16)
```

```python
import functools
import math

import jax
import jax.numpy as jnp
import numpy as np
from jax import lax
from jax.experimental import pallas as pl
from jax.experimental.pallas import tpu as pltpu
from jax.sharding import PartitionSpec as P

CH = 1536
DELAYS = 128
NBAND = 8
GPO = 2
CAP = 8


def fourier_tables(length):
    sample_index = np.arange(length, dtype=np.int32)
    phase_index = sample_index[:, None] * sample_index[None, :] % length
    angles = phase_index.astype(np.float32) * np.float32(2.0 * math.pi / length)
    cosine = np.cos(angles)
    sine_table = np.sin(angles)
    forward = np.concatenate(
        [np.concatenate([cosine, -sine_table], 1), np.concatenate([sine_table, cosine], 1)], 0
    )
    return forward.astype(jnp.bfloat16)


def band_response(band, length, band_count):
    mode_index = jnp.arange(length, dtype=jnp.int32)
    signed_modes = (mode_index - length * (mode_index >= length // 2).astype(jnp.int32)).astype(
        jnp.float32
    )
    center = (band.astype(jnp.float32) - (band_count - 1) / 2.0) * (length / (4.0 * band_count))
    band_width = length / 32.0
    offset_ratio = (signed_modes[None, :] - center[:, None]) / band_width
    single = (0.15 + 0.85 / (1.0 + offset_ratio**4)) / length
    return jnp.concatenate([single, single], 1)


def make_basis(channels, modes):
    channel_index = np.arange(channels, dtype=np.int32)
    order_index = np.arange(modes, dtype=np.int32)
    phase_index = order_index[None, :] * (2 * channel_index[:, None] + 1) % (4 * channels)
    return np.cos(phase_index.astype(np.float32) * np.float32(math.pi / (2 * channels))).astype(
        jnp.bfloat16
    )


NT = (((1,), (1,)), ((), ()))
BIG = 48 * 1024 * 1024


def dot32(left, right):
    return jnp.dot(left, right, preferred_element_type=jnp.float32)


def halves(value):
    high = value.astype(jnp.bfloat16)
    return high, (value - high.astype(jnp.float32)).astype(jnp.bfloat16)


def dot_split(left, right):
    left_high, left_low = left
    right_high, right_low = right
    return dot32(left_high, right_high) + (
        dot32(left_high, right_low) + dot32(left_low, right_high)
    )


def filter_kernel(shards, chunks, vis_ref, fwd_ref, inv_ref, resp_ref, weight_ref, basis_ref,
                  fringe_ref, proj_ref):
    batch, half = vis_ref.shape[0], vis_ref.shape[3]
    spectra = [
        dot32(vis_ref[i, :, 0, :], fwd_ref[:half]) + dot32(vis_ref[i, :, 1, :], fwd_ref[half:])
        for i in range(batch)
    ]
    spectra = [(spectra[i] * resp_ref[i]).astype(jnp.bfloat16) for i in range(batch)]
    for i in range(batch):
        fringe = lax.dot_general(inv_ref[...], spectra[i], NT, preferred_element_type=jnp.float32)
        fringe = (fringe * weight_ref[i]).astype(jnp.bfloat16)
        fringe_ref[i] = fringe
        projected = dot32(fringe, basis_ref[...])
        size = projected.shape[0] // chunks
        for h in range(chunks):
            piece = projected[h * size:(h + 1) * size].reshape(shards, -1, projected.shape[1])
            proj_ref[:, i, h] = piece.astype(jnp.bfloat16)


def inverse_kernel(batch, ridge, scales, start, weight_ref, basis_ref, basis_t_ref, out_ref):
    modes = out_ref.shape[1]
    eye = (
        lax.broadcasted_iota(jnp.int32, (modes, modes), 0)
        == lax.broadcasted_iota(jnp.int32, (modes, modes), 1)
    ).astype(jnp.float32)
    normals = [
        dot32(basis_t_ref[...] * weight_ref[i], basis_ref[...]) + ridge * eye for i in range(batch)
    ]
    first = scales[0]
    guess = [first * (2.0 * start * eye - start * start * normal) for normal in normals]
    normals = [halves(normal) for normal in normals]
    for scale in scales[1:]:
        guess_parts = [halves(value) for value in guess]
        product = [dot_split(n, g) for n, g in zip(normals, guess_parts)]
        change = [halves(2.0 * eye - value) for value in product]
        guess = [scale * dot_split(g, c) for g, c in zip(guess_parts, change)]
    for i in range(batch):
        out_ref[i] = guess[i]


def solve_kernel(batch, recv_ref, inverse_ref, *out_refs):
    for i in range(batch):
        inverse = halves(inverse_ref[i])
        for h, out_ref in enumerate(out_refs):
            total = jnp.sum(recv_ref[:, i, h].astype(jnp.float32), axis=0)
            out_ref[0, i] = dot_split(halves(total), inverse).astype(jnp.bfloat16)


def chain_kernel(shards, chunks, own_ref, out_ref, send_sem, recv_sem):
    me = lax.axis_index("freq")
    has_right, has_left = me < shards - 1, me > 0
    barrier = pltpu.get_barrier_semaphore()

    def greet(has, step):
        @pl.when(has)
        def _():
            pl.semaphore_signal(
                barrier, inc=1, device_id={"freq": me + step},
                device_id_type=pl.DeviceIdType.MESH,
            )

    greet(has_right, 1)
    greet(has_left, -1)
    pl.semaphore_wait(barrier, has_right.astype(jnp.int32) + has_left.astype(jnp.int32))

    def copy(way, h, hop, step):
        source = me - step * hop
        start = own_ref.at[h] if hop == 0 else out_ref.at[h, source]
        return pltpu.make_async_remote_copy(
            src_ref=start,
            dst_ref=out_ref.at[h, source],
            send_sem=send_sem.at[way, h, hop],
            recv_sem=recv_sem.at[way, h, hop],
            device_id={"freq": me + step},
            device_id_type=pl.DeviceIdType.MESH,
        )

    def arrival(way, h, hop, step):
        source = me - step * (hop + 1)
        return pltpu.make_async_remote_copy(
            src_ref=own_ref.at[h],
            dst_ref=out_ref.at[h, source],
            send_sem=send_sem.at[way, h, hop],
            recv_sem=recv_sem.at[way, h, hop],
            device_id={"freq": me - step},
            device_id_type=pl.DeviceIdType.MESH,
        )

    ways = ((0, 1, has_right), (1, -1, has_left))
    for hop in range(shards):
        for h in range(chunks):
            for way, step, has in ways:
                source = me - step * hop
                held = jnp.logical_and(source >= 0, source <= shards - 1)
                if hop > 0:
                    @pl.when(held)
                    def _():
                        arrival(way, h, hop - 1, step).wait_recv()
                if hop < shards - 1:
                    @pl.when(jnp.logical_and(held, has))
                    def _():
                        copy(way, h, hop, step).start()
        if hop == 0:
            for h in range(chunks):
                out_ref[h, me] = own_ref[h]
    for hop in range(shards - 1):
        for h in range(chunks):
            for way, step, has in ways:
                source = me - step * hop
                held = jnp.logical_and(source >= 0, source <= shards - 1)

                @pl.when(jnp.logical_and(held, has))
                def _():
                    copy(way, h, hop, step).wait_send()


def gather_chain(part, shards, chunks, call):
    if shards > 8:
        return jnp.stack([lax.all_gather(part[h], "freq") for h in range(chunks)])
    hops = max(shards - 1, 1)
    return pl.pallas_call(
        functools.partial(chain_kernel, shards, chunks),
        in_specs=[pl.BlockSpec(memory_space=pltpu.VMEM)],
        out_specs=pl.BlockSpec(memory_space=pltpu.VMEM),
        out_shape=jax.ShapeDtypeStruct((chunks, shards) + part.shape[1:], part.dtype),
        scratch_shapes=[
            pltpu.SemaphoreType.DMA((2, chunks, hops)),
            pltpu.SemaphoreType.DMA((2, chunks, hops)),
        ],
        compiler_params=pltpu.CompilerParams(
            collective_id=call, has_side_effects=True, vmem_limit_bytes=BIG
        ),
        cost_estimate=pl.CostEstimate(
            flops=20_000_000_000, bytes_accessed=2 * shards * part.size, transcendentals=0
        ),
    )(part)


def clean_kernel(ids_ref, fringe_ref, coef_ref, basis_t_ref, weight_ref, out_ref, total_ref):
    item = pl.program_id(0)

    @pl.when(item == 0)
    def _():
        total_ref[...] = jnp.zeros_like(total_ref)

    batch, size = fringe_ref.shape[0], fringe_ref.shape[1]
    for i in range(batch):
        coef = coef_ref[0, :, i].astype(jnp.float32)
        coef = coef.reshape(-1, coef.shape[2]).astype(jnp.bfloat16)
        fitted = dot32(coef, basis_t_ref[...]) * weight_ref[i]
        group = ids_ref[item * batch + i]
        total_ref[group, :size] += fringe_ref[i].astype(jnp.float32) - fitted
        total_ref[group, size:] += jnp.ones_like(total_ref[group, size:])

    @pl.when(item == pl.num_programs(0) - 1)
    def _():
        out_ref[...] = total_ref[...].astype(jnp.bfloat16)


def newton_scales(low, high):
    scales = []
    value = (high + low) / (high - low)
    while True:
        doubled = 2.0 * value * value
        scales.append(doubled / (doubled - 1.0))
        value = doubled - 1.0
        if value > 1e6:
            return scales


def full(shape):
    return pl.BlockSpec(shape, lambda i, *rest: (0,) * len(shape))


def lead(shape):
    return pl.BlockSpec(shape, lambda i, *rest: (i,) + (0,) * (len(shape) - 1))


def second(shape):
    return pl.BlockSpec(shape, lambda i, *rest: (0, i) + (0,) * (len(shape) - 2))


def per_device_general(vis, flags, band, group_id):
    items, chan, _, length = vis.shape
    both = 2 * length
    shards = lax.axis_size("freq")
    owners = lax.axis_size("bl")
    groups = GPO * owners
    time_local = length // shards
    rows = 2 * time_local
    pair = 2 if items % 2 == 0 else 1
    chunks = 2 if rows % 32 == 0 else 1
    rows //= chunks
    size = both // chunks
    bf16, f32 = jnp.bfloat16, jnp.float32

    table = fourier_tables(length)
    forward = jnp.asarray(table)
    inverse_t = forward
    if chunks == 1:
        inverse_t = table.reshape(2, shards, time_local, both)
        inverse_t = jnp.asarray(np.transpose(inverse_t, (1, 0, 2, 3)).reshape(both, both))
    response = band_response(band, length, NBAND).reshape(items, 1, both)
    basis = make_basis(CH, DELAYS)
    basis_t = jnp.asarray(basis.T.copy())
    basis = jnp.asarray(basis)
    basis_local = lax.dynamic_slice_in_dim(basis, lax.axis_index("freq") * chan, chan, 0)
    weight = 1.0 - flags.astype(f32)
    weight_rows = weight.reshape(items, 1, chan)
    weight_half = weight.astype(bf16)
    if shards <= 8:
        pieces = [weight_half] + [
            lax.ppermute(weight_half, "freq", [(d, (d - j) % shards) for d in range(shards)])
            for j in range(1, shards)
        ]
        doubled = jnp.concatenate(pieces + pieces, axis=1)
        offset = (shards - lax.axis_index("freq")) % shards * chan
        weight_full = lax.dynamic_slice_in_dim(doubled, offset, CH, 1)
    else:
        weight_full = lax.all_gather(weight_half, "freq", axis=1, tiled=True)
        response, weight_full = lax.optimization_barrier((response, weight_full))
    weight_full = weight_full.reshape(items, 1, CH)

    fringe, projected = pl.pallas_call(
        functools.partial(filter_kernel, shards, chunks),
        grid=(items // pair,),
        in_specs=[
            lead((pair, chan, 2, length)), full((both, both)), full((both, both)),
            lead((pair, 1, both)), lead((pair, 1, chan)), full((chan, DELAYS)),
        ],
        out_specs=[lead((pair, both, chan)), second((shards, pair, chunks, rows, DELAYS))],
        out_shape=[
            jax.ShapeDtypeStruct((items, both, chan), bf16),
            jax.ShapeDtypeStruct((shards, items, chunks, rows, DELAYS), bf16),
        ],
        compiler_params=pltpu.CompilerParams(vmem_limit_bytes=BIG),
        cost_estimate=pl.CostEstimate(
            flops=4 * items * chan * both * both, bytes_accessed=4 * items * chan * both,
            transcendentals=0,
        ),
    )(vis, forward, inverse_t, response, weight_rows, basis_local)

    projected, weight_full = lax.optimization_barrier((projected, weight_full))
    ridge = CH / 64.0
    high = ridge + 1.05 * CH
    batch = 4 if items % 4 == 0 else 1
    inverse = pl.pallas_call(
        functools.partial(
            inverse_kernel, batch, ridge, newton_scales(ridge, high), 2.0 / (ridge + high)
        ),
        grid=(items // batch,),
        in_specs=[lead((batch, 1, CH)), full((CH, DELAYS)), full((DELAYS, CH))],
        out_specs=lead((batch, DELAYS, DELAYS)),
        out_shape=jax.ShapeDtypeStruct((items, DELAYS, DELAYS), f32),
        compiler_params=pltpu.CompilerParams(vmem_limit_bytes=BIG),
        cost_estimate=pl.CostEstimate(
            flops=20_000_000_000, bytes_accessed=4 * items * DELAYS * DELAYS, transcendentals=0
        ),
    )(weight_full, basis, basis_t)

    received = lax.all_to_all(projected, "freq", split_axis=0, concat_axis=0, tiled=True)
    coefficients = pl.pallas_call(
        functools.partial(solve_kernel, batch),
        grid=(items // batch,),
        in_specs=[
            second((shards, batch, chunks, rows, DELAYS)), lead((batch, DELAYS, DELAYS)),
        ],
        out_specs=[second((1, batch, rows, DELAYS))] * chunks,
        out_shape=[jax.ShapeDtypeStruct((1, items, rows, DELAYS), bf16)] * chunks,
        compiler_params=pltpu.CompilerParams(vmem_limit_bytes=BIG),
    )(received, inverse)
    basis_local_t = basis_local.T
    tall = size + 16

    def clean(h, gathered):
        return pl.pallas_call(
            clean_kernel,
            grid_spec=pltpu.PrefetchScalarGridSpec(
                num_scalar_prefetch=1,
                grid=(items // batch,),
                in_specs=[
                    pl.BlockSpec((batch, size, chan), lambda i, ids: (i, h, 0)),
                    pl.BlockSpec((1, shards, batch, rows, DELAYS), lambda i, ids: (0, 0, i, 0, 0)),
                    full((DELAYS, chan)),
                    lead((batch, 1, chan)),
                ],
                out_specs=full((groups, tall, chan)),
                scratch_shapes=[pltpu.VMEM((groups, tall, chan), f32)],
            ),
            out_shape=jax.ShapeDtypeStruct((groups, tall, chan), bf16),
            compiler_params=pltpu.CompilerParams(vmem_limit_bytes=BIG),
            cost_estimate=pl.CostEstimate(
                flops=2_000_000_000, bytes_accessed=4 * items * size * chan, transcendentals=0
            ),
        )(group_id, fringe, gathered, basis_local_t, weight_rows)

    pieces = []
    for h in range(chunks):
        part = coefficients[h]
        if h:
            part, sums = lax.optimization_barrier((part, sums))
        sums = clean(h, gather_chain(part, shards, 1, h))
        if h:
            sums, pieces[-1] = lax.optimization_barrier((sums, pieces[-1]))
        arrived = lax.all_to_all(sums, "bl", split_axis=0, concat_axis=0, tiled=True)
        total = jnp.sum(arrived.reshape(owners, GPO, tall, chan).astype(f32), 0)
        counts = jnp.maximum(total[:, size:size + 1, :1], 1.0)
        mean = (total[:, :size] / counts).astype(bf16).reshape(GPO, shards, rows, chan)
        pieces.append(jnp.transpose(mean, (1, 0, 2, 3)))
    if shards > 8:
        swapped = [
            lax.all_to_all(piece, "freq", split_axis=0, concat_axis=0, tiled=True)
            for piece in pieces
        ]
        swapped = [jnp.concatenate(list(piece), axis=-1) for piece in swapped]
    else:
        me = lax.axis_index("freq")
        swapped = []
        for piece in pieces:
            parts = [lax.dynamic_index_in_dim(piece, me, 0, keepdims=False)]
            for j in range(1, shards):
                out = lax.dynamic_index_in_dim(piece, (me + shards - j) % shards, 0, keepdims=False)
                parts.append(
                    lax.ppermute(out, "freq", [(d, (d - j) % shards) for d in range(shards)])
                )
            doubled = jnp.concatenate(parts + parts, axis=-1)
            offset = (shards - me) % shards * chan
            swapped.append(lax.dynamic_slice_in_dim(doubled, offset, CH, 2))
    averaged = [piece.reshape(GPO, 2 // chunks, time_local, CH) for piece in swapped]
    return jnp.concatenate(averaged, 1)


MESH = pl.DeviceIdType.MESH
RANK = 48
PERM, BANDS, KEEP, LAST, SLOT, CODE = 0, 16, 32, 48, 56, 88


def filter_tables(length, shards):
    sample_index = np.arange(length)
    phase_index = sample_index[:, None] * sample_index[None, :] % length
    angles = phase_index.astype(np.float32) * np.float32(2.0 * math.pi / length)
    cosine = np.cos(angles).astype(jnp.bfloat16).astype(np.float64)
    sine = np.sin(angles).astype(jnp.bfloat16).astype(np.float64)
    signed = (sample_index - length * (sample_index >= length // 2)).astype(np.float64)
    tables = []
    for band in range(NBAND):
        center = (band - (NBAND - 1) / 2.0) * (length / (4.0 * NBAND))
        ratio = (signed - center) / (length / 32.0)
        response = (0.15 + 0.85 / (1.0 + ratio**4)) / length
        even = (cosine * response) @ cosine + (sine * response) @ sine
        odd = (cosine * response) @ sine - (sine * response) @ cosine
        whole = np.concatenate(
            [np.concatenate([even, odd], 1), np.concatenate([-odd, even], 1)], 0
        )
        tables.append(whole.T)
    tables = np.stack(tables).reshape(NBAND, 2, shards, length // shards, 2 * length)
    tables = np.transpose(tables, (0, 2, 1, 3, 4))
    return tables.reshape(NBAND, shards, 2 * length // shards, 2 * length).astype(jnp.bfloat16)


def factored_basis(channels, modes, shards):
    size = channels // shards
    channel_index = np.arange(channels)
    order_index = np.arange(modes)
    phase = (order_index[None, :] * (2 * channel_index[:, None] + 1) % (4 * channels)).astype(
        np.longdouble
    )
    exact = np.cos(phase * (np.longdouble(np.pi) / (2 * channels)))
    fronts, backs = [], []
    for z in range(shards):
        block = exact[z * size:(z + 1) * size]
        rest = block.copy()
        columns = []
        for _ in range(RANK):
            norms = (rest * rest).sum(0)
            best = int(np.argmax(norms))
            column = rest[:, best] / np.sqrt(norms[best])
            for other in columns:
                column = column - other * (other * column).sum()
            column = column / np.sqrt((column * column).sum())
            columns.append(column)
            rest = rest - column[:, None] * (column[:, None] * rest).sum(0)[None]
        front = np.stack(columns)
        fronts.append(front)
        backs.append(np.stack([(row[:, None] * block).sum(0) for row in front]))
    fronts = np.stack(fronts).astype(np.float32).astype(jnp.bfloat16)
    backs = np.concatenate(backs).astype(np.float32).astype(jnp.bfloat16)
    return fronts, backs.T.copy()


def plan_kernel(ids_ref, band_ref, flags_ref, meta_ref, half_ref, rows_ref, count_ref, begin_ref,
                sorted_ref):
    items = flags_ref.shape[0]
    groups = count_ref.shape[0]
    owners = groups // GPO
    for g in range(groups):
        count_ref[g] = 0
    for b in range(items):
        g = ids_ref[b]
        count_ref[g] = count_ref[g] + 1
    total = 0
    for g in range(groups):
        begin_ref[g] = total
        total = total + count_ref[g]
        meta_ref[LAST + g] = jnp.where(count_ref[g] > 0, total, 0)
    for o in range(owners):
        first = begin_ref[GPO * o]
        middle = begin_ref[GPO * o + 1]
        end = middle + count_ref[GPO * o + 1]
        for s in range(CAP):
            place = first + s
            used = place < end
            meta_ref[SLOT + o * CAP + s] = jnp.where(used, place, items)
            meta_ref[CODE + o * CAP + s] = jnp.where(
                used, jnp.where(place < middle, 1, 2), 0
            )
    for b in range(items):
        g = ids_ref[b]
        place = begin_ref[g]
        begin_ref[g] = place + 1
        meta_ref[PERM + place] = b
        meta_ref[BANDS + place] = band_ref[b]
        sorted_ref[place] = g
    meta_ref[KEEP] = 0
    for p in range(1, items):
        meta_ref[KEEP + p] = (sorted_ref[p] == sorted_ref[p - 1]).astype(jnp.int32)
    for p in range(items):
        row = flags_ref[pl.ds(meta_ref[PERM + p], 1), :]
        rows_ref[p:p + 1, :] = 1.0 - row.astype(jnp.float32)
    half_ref[...] = rows_ref[...].astype(jnp.bfloat16)


def dot_nt(left, right):
    return lax.dot_general(left, right, NT, preferred_element_type=jnp.float32)


def main_kernel(ridge, scales, start_scale, meta, vis_hbm, half_ref, rows_ref, m_hbm, front_ref,
                back_ref, basis_hbm, basis_t_hbm, out_ref,
                vis_v, m_0, m_1, m_2, m_3, basis_v, basis_t_v, sep, sums, own_keep, pass_keep,
                pair_send, pair_recv, cross_send, cross_recv, far_send, far_recv,
                y_send, y_recv, w_recv, wide, inv_v, coef_v, coef_send, coef_recv,
                code_tmp, code_send, code_recv, left_v, right_v, fit_v,
                local_sem, send_sem, recv_sem):
    f32, bf16 = jnp.float32, jnp.bfloat16
    items, chan = vis_v.shape[0], vis_v.shape[1]
    length = vis_v.shape[3]
    m_v = (m_0, m_1, m_2, m_3)
    rt = m_0.shape[1]
    modes = basis_v.shape[1]
    me_b, me_f = lax.axis_index("bl"), lax.axis_index("freq")
    me_x, me_c = me_b // 2, lax.rem(me_b, 2)
    far = [lax.rem(me_f + 2, 4), 3 - me_f, me_f + 1 - 2 * lax.rem(me_f, 2), me_f]
    sibling = me_b + 1 - 2 * me_c
    across = lax.rem(me_b + 2, 4)
    diagonal = 3 - me_b
    owners = [me_b, sibling, across, diagonal]

    chunk = items // 4
    loads = [
        pltpu.make_async_copy(
            vis_hbm.at[pl.ds(i * chunk, chunk)], vis_v.at[pl.ds(i * chunk, chunk)],
            local_sem.at[i],
        )
        for i in range(4)
    ]
    tables = [
        pltpu.make_async_copy(m_hbm.at[:, far[j]], m_v[j], local_sem.at[4 + j])
        for j in range(4)
    ]
    bases = [
        pltpu.make_async_copy(basis_hbm, basis_v, local_sem.at[8]),
        pltpu.make_async_copy(basis_t_hbm, basis_t_v, local_sem.at[9]),
    ]
    for copy in [loads[0], tables[0]] + loads[1:] + tables[1:] + bases:
        copy.start()

    barrier = pltpu.get_barrier_semaphore()
    for j in range(3):
        pl.semaphore_signal(barrier, inc=1, device_id={"freq": far[j]}, device_id_type=MESH)
        pl.semaphore_signal(barrier, inc=1, device_id={"bl": owners[j + 1]}, device_id_type=MESH)
    pl.semaphore_wait(barrier, 6)

    pending = []

    def send(index, source, target, axis, place):
        copy = pltpu.make_async_remote_copy(
            src_ref=source, dst_ref=target, send_sem=send_sem.at[index],
            recv_sem=recv_sem.at[index], device_id={axis: place}, device_id_type=MESH,
        )
        copy.start()
        pending.append(copy)
        return copy

    w_copies = [send(j, half_ref, w_recv.at[me_f], "freq", far[j]) for j in range(3)]

    sums[0] = jnp.zeros_like(sums[0])
    for i in range(4):
        loads[i].wait()

        def separate(b, carry):
            sep[b, :, :length] = vis_v[b, :, 0, :]
            sep[b, :, length:] = vis_v[b, :, 1, :]
            return carry

        lax.fori_loop(i * chunk, (i + 1) * chunk, separate, 0, unroll=2)

    y_copies, pair_copies, cross_copies, far_copies = [], [], [], []

    def pair_stage(j):
        pair_copies[j].wait_recv()
        for l in range(GPO):
            passed = pass_keep[j, l] + pair_recv[j, GPO * (1 - me_x) + l].astype(f32)
            cross_send[j, l] = passed.astype(bf16)
            own_keep[j, l] = own_keep[j, l] + pair_recv[j, GPO * me_x + l].astype(f32)
        cross_copies.append(send(10 + j, cross_send.at[j], cross_recv.at[j], "bl", across))

    def cross_stage(j):
        cross_copies[j].wait_recv()
        total = (own_keep[j] + cross_recv[j].astype(f32)).astype(bf16)
        if j < 3:
            far_send[j] = total
            far_copies.append(send(14 + j, far_send.at[j], far_recv.at[me_f], "freq", far[j]))
        else:
            far_recv[me_f] = total

    for j in range(4):
        tables[j].wait()

        def one(p, carry):
            table = m_v[j][meta[BANDS + p]]
            fringe = dot_nt(table, sep[meta[PERM + p]]) * rows_ref[pl.ds(p, 1), :]
            keep = meta[KEEP + p].astype(f32)
            sums[p + 1] = sums[p] * keep + fringe
            y = dot_nt(front_ref[me_f], fringe.astype(bf16)).astype(bf16)
            if j < 3:
                y_send[j, p] = y
            else:
                y_recv[me_f, p] = y
            return carry

        lax.fori_loop(0, items, one, 0, unroll=4)
        if j < 3:
            y_copies.append(send(3 + j, y_send.at[j], y_recv.at[me_f], "freq", far[j]))
        for x in range(2):
            for l in range(GPO):
                group = GPO * (2 * x + 1 - me_c) + l
                pair_send[j, GPO * x + l] = sums[meta[LAST + group]].astype(bf16)
        pair_copies.append(send(6 + j, pair_send.at[j], pair_recv.at[j], "bl", sibling))
        for l in range(GPO):
            own_keep[j, l] = sums[meta[LAST + GPO * me_b + l]]
            pass_keep[j, l] = sums[meta[LAST + GPO * across + l]]
        if j > 0:
            pair_stage(j - 1)
    pair_stage(3)

    for copy in w_copies:
        copy.wait_recv()
    w_recv[me_f] = half_ref[...]
    for z in range(4):
        wide[:items, z * chan:(z + 1) * chan] = w_recv[z].astype(f32)
    wide[items:, :] = jnp.zeros_like(wide[items:, :])

    half = wide.shape[1] // 2
    code_copies = []
    for k in range(4):
        for s in range(CAP):
            code = meta[CODE + owners[k] * CAP + s].astype(f32)
            row = wide[pl.ds(meta[SLOT + owners[k] * CAP + s], 1), :] * code
            for h in range(2):
                code_tmp[h * CAP + s:h * CAP + s + 1, :half] = row[:, h * half:(h + 1) * half]
                code_tmp[h * CAP + s:h * CAP + s + 1, half:] = (
                    jnp.zeros((1, code_tmp.shape[1] - half), f32) + code
                )
        if k == 0:
            code_recv[me_b] = code_tmp[...].astype(bf16)
        else:
            code_send[k - 1] = code_tmp[...].astype(bf16)
            code_copies.append(
                send(16 + k, code_send.at[k - 1], code_recv.at[me_b], "bl", owners[k])
            )

    for copy in bases:
        copy.wait()
    eye = (
        lax.broadcasted_iota(jnp.int32, (modes, modes), 0)
        == lax.broadcasted_iota(jnp.int32, (modes, modes), 1)
    ).astype(f32)
    batch = 4

    def invert(step, carry):
        normals = []
        for i in range(batch):
            weight = wide[pl.ds(step * batch + i, 1), :].astype(bf16)
            normals.append(dot32(basis_t_v[...] * weight, basis_v[...]) + ridge * eye)
        guess = [
            scales[0] * (2.0 * start_scale * eye - start_scale * start_scale * normal)
            for normal in normals
        ]
        normals = [halves(normal) for normal in normals]
        for scale in scales[1:]:
            guess_parts = [halves(value) for value in guess]
            product = [dot_split(n, g) for n, g in zip(normals, guess_parts)]
            change = [halves(2.0 * eye - value) for value in product]
            guess = [scale * dot_split(g, c) for g, c in zip(guess_parts, change)]
        for i in range(batch):
            inv_v[step * batch + i] = guess[i]
        return carry

    for j in range(4):
        lax.fori_loop(j, j + 1, invert, 0)
        cross_stage(j)

    for copy in y_copies:
        copy.wait_recv()

    def solve(p, carry):
        values = y_recv[:, p].reshape(-1, rt)
        projected = dot32(back_ref[...], values).T
        coef_v[p] = dot_split(halves(projected), halves(inv_v[p])).astype(bf16)
        return carry

    lax.fori_loop(0, items, solve, 0, unroll=4)
    coef_v[items] = jnp.zeros_like(coef_v[items])
    coef_copies = []
    for k in (2, 3, 1, 0):
        for s in range(CAP):
            value = coef_v[meta[SLOT + owners[k] * CAP + s]]
            if k == 0:
                coef_recv[me_b, s] = value
            else:
                coef_send[k - 1, s] = value
        if k > 0:
            coef_copies.append(
                send(19 + k, coef_send.at[k - 1], coef_recv.at[me_b], "bl", owners[k])
            )

    counts = [jnp.zeros((1, 128), f32) for _ in range(GPO)]
    for k in range(4):
        if k > 0:
            code_copies[k - 1].wait_recv()
            coef_copies[{1: 2, 2: 0, 3: 1}[k]].wait_recv()
        place = owners[k]
        codes = code_recv[place].astype(f32)
        for s in range(CAP):
            value = coef_recv[place, s].astype(f32)
            for l in range(GPO):
                match = (codes[s:s + 1, half:half + 128] == 1.0 + l).astype(f32)
                counts[l] = counts[l] + match
                left_v[l * rt:(l + 1) * rt, s * modes:(s + 1) * modes] = (value * match).astype(
                    bf16
                )
        for h in range(2):
            for s in range(CAP):
                row = codes[h * CAP + s:h * CAP + s + 1, :half]
                weight = (row > 0.0).astype(f32).astype(bf16)
                right_v[s * modes:(s + 1) * modes, :] = (
                    basis_t_v[:, h * half:(h + 1) * half] * weight
                )
            fitted = dot32(left_v[...], right_v[...])
            if k == 0:
                fit_v[:, h * half:(h + 1) * half] = fitted
            else:
                fit_v[:, h * half:(h + 1) * half] = fit_v[:, h * half:(h + 1) * half] + fitted

    for copy in far_copies:
        copy.wait_recv()
    for l in range(GPO):
        scale = 1.0 / jnp.maximum(counts[l][:, :1], 1.0)
        for z in range(4):
            rest = far_recv[z, l].astype(f32) - fit_v[l * rt:(l + 1) * rt, z * chan:(z + 1) * chan]
            out_ref[l, :, z * chan:(z + 1) * chan] = (rest * scale).astype(bf16)
    for copy in pending:
        copy.wait_send()


def per_device_fused(vis, flags, band, group_id):
    items, chan, _, length = vis.shape
    shards = 4
    f32, bf16 = jnp.float32, jnp.bfloat16
    rt = 2 * length // shards
    channels = chan * shards
    smem = pl.BlockSpec(memory_space=pltpu.SMEM)
    vmem = pl.BlockSpec(memory_space=pltpu.VMEM)
    hbm = pl.BlockSpec(memory_space=pl.ANY)
    meta, weight_half, weight_rows = pl.pallas_call(
        plan_kernel,
        in_specs=[smem, smem, vmem],
        out_specs=[smem, vmem, vmem],
        out_shape=[
            jax.ShapeDtypeStruct((128,), jnp.int32),
            jax.ShapeDtypeStruct((items, chan), bf16),
            jax.ShapeDtypeStruct((items, chan), f32),
        ],
        scratch_shapes=[
            pltpu.SMEM((GPO * 4,), jnp.int32), pltpu.SMEM((GPO * 4,), jnp.int32),
            pltpu.SMEM((items,), jnp.int32),
        ],
    )(group_id, band, flags)
    table = jnp.asarray(filter_tables(length, shards))
    fronts, backs = factored_basis(channels, DELAYS, shards)
    basis = make_basis(channels, DELAYS)
    ridge = channels / 64.0
    high = ridge + 1.05 * channels
    half = channels // 2
    out = pl.pallas_call(
        functools.partial(main_kernel, ridge, newton_scales(ridge, high), 2.0 / (ridge + high)),
        in_specs=[smem, hbm, vmem, vmem, hbm, vmem, vmem, hbm, hbm],
        out_specs=vmem,
        out_shape=jax.ShapeDtypeStruct((GPO, rt, channels), bf16),
        scratch_shapes=[
            pltpu.VMEM(vis.shape, bf16),
            pltpu.VMEM((NBAND, rt, 2 * length), bf16),
            pltpu.VMEM((NBAND, rt, 2 * length), bf16),
            pltpu.VMEM((NBAND, rt, 2 * length), bf16),
            pltpu.VMEM((NBAND, rt, 2 * length), bf16),
            pltpu.VMEM((channels, DELAYS), bf16),
            pltpu.VMEM((DELAYS, channels), bf16),
            pltpu.VMEM((items, chan, 2 * length), bf16),
            pltpu.VMEM((items + 1, rt, chan), f32),
            pltpu.VMEM((4, GPO, rt, chan), f32),
            pltpu.VMEM((4, GPO, rt, chan), f32),
            pltpu.VMEM((4, 2 * GPO, rt, chan), bf16),
            pltpu.VMEM((4, 2 * GPO, rt, chan), bf16),
            pltpu.VMEM((4, GPO, rt, chan), bf16),
            pltpu.VMEM((4, GPO, rt, chan), bf16),
            pltpu.VMEM((3, GPO, rt, chan), bf16),
            pltpu.VMEM((shards, GPO, rt, chan), bf16),
            pltpu.VMEM((3, items, RANK, rt), bf16),
            pltpu.VMEM((shards, items, RANK, rt), bf16),
            pltpu.VMEM((shards, items, chan), bf16),
            pltpu.VMEM((items + 8, channels), f32),
            pltpu.VMEM((items, DELAYS, DELAYS), f32),
            pltpu.VMEM((items + 1, rt, DELAYS), bf16),
            pltpu.VMEM((3, CAP, rt, DELAYS), bf16),
            pltpu.VMEM((4, CAP, rt, DELAYS), bf16),
            pltpu.VMEM((2 * CAP, half + 128), f32),
            pltpu.VMEM((3, 2 * CAP, half + 128), bf16),
            pltpu.VMEM((4, 2 * CAP, half + 128), bf16),
            pltpu.VMEM((GPO * rt, CAP * DELAYS), bf16),
            pltpu.VMEM((CAP * DELAYS, half), bf16),
            pltpu.VMEM((GPO * rt, channels), f32),
            pltpu.SemaphoreType.DMA((10,)),
            pltpu.SemaphoreType.DMA((23,)),
            pltpu.SemaphoreType.DMA((23,)),
        ],
        compiler_params=pltpu.CompilerParams(
            collective_id=0, has_side_effects=True, vmem_limit_bytes=58 * 1024 * 1024
        ),
        cost_estimate=pl.CostEstimate(
            flops=10_000_000_000, bytes_accessed=4 * vis.size, transcendentals=0
        ),
    )(
        meta, vis, weight_half, weight_rows, table, jnp.asarray(fronts), jnp.asarray(backs),
        jnp.asarray(basis), jnp.asarray(basis.T.copy()),
    )
    return out.reshape(GPO, 2, length // shards, channels)


def per_device(vis, flags, band, group_id):
    items, chan, _, length = vis.shape
    fits = (
        lax.axis_size("freq") == 4 and lax.axis_size("bl") == 4 and items == 16
        and chan % 128 == 0 and length == 256
    )
    return (per_device_fused if fits else per_device_general)(vis, flags, band, group_id)


def solution(mesh):
    in_specs = (P("bl", "freq", None, "win"), P("bl", "freq"), P("bl"), P("bl"))
    out_specs = P("bl", None, ("win", "freq"), None)
    return jax.shard_map(
        per_device, mesh=mesh, in_specs=in_specs, out_specs=out_specs, check_vma=False
    )
```

```python
import functools
import math

import jax
import jax.numpy as jnp
import numpy as np
from jax import lax
from jax.experimental import pallas as pl
from jax.experimental.pallas import tpu as pltpu
from jax.sharding import PartitionSpec as P

CH = 1536
DELAYS = 128
NBAND = 8
GPO = 2
CAP = 8


def fourier_tables(length):
    sample_index = np.arange(length, dtype=np.int32)
    phase_index = sample_index[:, None] * sample_index[None, :] % length
    angles = phase_index.astype(np.float32) * np.float32(2.0 * math.pi / length)
    cosine = np.cos(angles)
    sine_table = np.sin(angles)
    forward = np.concatenate(
        [np.concatenate([cosine, -sine_table], 1), np.concatenate([sine_table, cosine], 1)], 0
    )
    return forward.astype(jnp.bfloat16)


def band_response(band, length, band_count):
    mode_index = jnp.arange(length, dtype=jnp.int32)
    signed_modes = (mode_index - length * (mode_index >= length // 2).astype(jnp.int32)).astype(
        jnp.float32
    )
    center = (band.astype(jnp.float32) - (band_count - 1) / 2.0) * (length / (4.0 * band_count))
    band_width = length / 32.0
    offset_ratio = (signed_modes[None, :] - center[:, None]) / band_width
    single = (0.15 + 0.85 / (1.0 + offset_ratio**4)) / length
    return jnp.concatenate([single, single], 1)


def make_basis(channels, modes):
    channel_index = np.arange(channels, dtype=np.int32)
    order_index = np.arange(modes, dtype=np.int32)
    phase_index = order_index[None, :] * (2 * channel_index[:, None] + 1) % (4 * channels)
    return np.cos(phase_index.astype(np.float32) * np.float32(math.pi / (2 * channels))).astype(
        jnp.bfloat16
    )


NT = (((1,), (1,)), ((), ()))
BIG = 48 * 1024 * 1024


def dot32(left, right):
    return jnp.dot(left, right, preferred_element_type=jnp.float32)


def halves(value):
    high = value.astype(jnp.bfloat16)
    return high, (value - high.astype(jnp.float32)).astype(jnp.bfloat16)


def dot_split(left, right):
    left_high, left_low = left
    right_high, right_low = right
    return dot32(left_high, right_high) + (
        dot32(left_high, right_low) + dot32(left_low, right_high)
    )


def filter_kernel(shards, chunks, vis_ref, fwd_ref, inv_ref, resp_ref, weight_ref, basis_ref,
                  fringe_ref, proj_ref):
    batch, half = vis_ref.shape[0], vis_ref.shape[3]
    spectra = [
        dot32(vis_ref[i, :, 0, :], fwd_ref[:half]) + dot32(vis_ref[i, :, 1, :], fwd_ref[half:])
        for i in range(batch)
    ]
    spectra = [(spectra[i] * resp_ref[i]).astype(jnp.bfloat16) for i in range(batch)]
    for i in range(batch):
        fringe = lax.dot_general(inv_ref[...], spectra[i], NT, preferred_element_type=jnp.float32)
        fringe = (fringe * weight_ref[i]).astype(jnp.bfloat16)
        fringe_ref[i] = fringe
        projected = dot32(fringe, basis_ref[...])
        size = projected.shape[0] // chunks
        for h in range(chunks):
            piece = projected[h * size:(h + 1) * size].reshape(shards, -1, projected.shape[1])
            proj_ref[:, i, h] = piece.astype(jnp.bfloat16)


def inverse_kernel(batch, ridge, scales, start, weight_ref, basis_ref, basis_t_ref, out_ref):
    modes = out_ref.shape[1]
    eye = (
        lax.broadcasted_iota(jnp.int32, (modes, modes), 0)
        == lax.broadcasted_iota(jnp.int32, (modes, modes), 1)
    ).astype(jnp.float32)
    normals = [
        dot32(basis_t_ref[...] * weight_ref[i], basis_ref[...]) + ridge * eye for i in range(batch)
    ]
    first = scales[0]
    guess = [first * (2.0 * start * eye - start * start * normal) for normal in normals]
    normals = [halves(normal) for normal in normals]
    for scale in scales[1:]:
        guess_parts = [halves(value) for value in guess]
        product = [dot_split(n, g) for n, g in zip(normals, guess_parts)]
        change = [halves(2.0 * eye - value) for value in product]
        guess = [scale * dot_split(g, c) for g, c in zip(guess_parts, change)]
    for i in range(batch):
        out_ref[i] = guess[i]


def solve_kernel(batch, recv_ref, inverse_ref, *out_refs):
    for i in range(batch):
        inverse = halves(inverse_ref[i])
        for h, out_ref in enumerate(out_refs):
            total = jnp.sum(recv_ref[:, i, h].astype(jnp.float32), axis=0)
            out_ref[0, i] = dot_split(halves(total), inverse).astype(jnp.bfloat16)


def chain_kernel(shards, chunks, own_ref, out_ref, send_sem, recv_sem):
    me = lax.axis_index("freq")
    has_right, has_left = me < shards - 1, me > 0
    barrier = pltpu.get_barrier_semaphore()

    def greet(has, step):
        @pl.when(has)
        def _():
            pl.semaphore_signal(
                barrier, inc=1, device_id={"freq": me + step},
                device_id_type=pl.DeviceIdType.MESH,
            )

    greet(has_right, 1)
    greet(has_left, -1)
    pl.semaphore_wait(barrier, has_right.astype(jnp.int32) + has_left.astype(jnp.int32))

    def copy(way, h, hop, step):
        source = me - step * hop
        start = own_ref.at[h] if hop == 0 else out_ref.at[h, source]
        return pltpu.make_async_remote_copy(
            src_ref=start,
            dst_ref=out_ref.at[h, source],
            send_sem=send_sem.at[way, h, hop],
            recv_sem=recv_sem.at[way, h, hop],
            device_id={"freq": me + step},
            device_id_type=pl.DeviceIdType.MESH,
        )

    def arrival(way, h, hop, step):
        source = me - step * (hop + 1)
        return pltpu.make_async_remote_copy(
            src_ref=own_ref.at[h],
            dst_ref=out_ref.at[h, source],
            send_sem=send_sem.at[way, h, hop],
            recv_sem=recv_sem.at[way, h, hop],
            device_id={"freq": me - step},
            device_id_type=pl.DeviceIdType.MESH,
        )

    ways = ((0, 1, has_right), (1, -1, has_left))
    for hop in range(shards):
        for h in range(chunks):
            for way, step, has in ways:
                source = me - step * hop
                held = jnp.logical_and(source >= 0, source <= shards - 1)
                if hop > 0:
                    @pl.when(held)
                    def _():
                        arrival(way, h, hop - 1, step).wait_recv()
                if hop < shards - 1:
                    @pl.when(jnp.logical_and(held, has))
                    def _():
                        copy(way, h, hop, step).start()
        if hop == 0:
            for h in range(chunks):
                out_ref[h, me] = own_ref[h]
    for hop in range(shards - 1):
        for h in range(chunks):
            for way, step, has in ways:
                source = me - step * hop
                held = jnp.logical_and(source >= 0, source <= shards - 1)

                @pl.when(jnp.logical_and(held, has))
                def _():
                    copy(way, h, hop, step).wait_send()


def gather_chain(part, shards, chunks, call):
    if shards > 8:
        return jnp.stack([lax.all_gather(part[h], "freq") for h in range(chunks)])
    hops = max(shards - 1, 1)
    return pl.pallas_call(
        functools.partial(chain_kernel, shards, chunks),
        in_specs=[pl.BlockSpec(memory_space=pltpu.VMEM)],
        out_specs=pl.BlockSpec(memory_space=pltpu.VMEM),
        out_shape=jax.ShapeDtypeStruct((chunks, shards) + part.shape[1:], part.dtype),
        scratch_shapes=[
            pltpu.SemaphoreType.DMA((2, chunks, hops)),
            pltpu.SemaphoreType.DMA((2, chunks, hops)),
        ],
        compiler_params=pltpu.CompilerParams(
            collective_id=call, has_side_effects=True, vmem_limit_bytes=58 * 1024 * 1024
        ),
        cost_estimate=pl.CostEstimate(
            flops=20_000_000_000, bytes_accessed=2 * shards * part.size, transcendentals=0
        ),
    )(part)


def clean_kernel(ids_ref, fringe_ref, coef_ref, basis_t_ref, weight_ref, out_ref, total_ref):
    item = pl.program_id(0)

    @pl.when(item == 0)
    def _():
        total_ref[...] = jnp.zeros_like(total_ref)

    batch, size = fringe_ref.shape[0], fringe_ref.shape[1]
    for i in range(batch):
        coef = coef_ref[0, :, i].astype(jnp.float32)
        coef = coef.reshape(-1, coef.shape[2]).astype(jnp.bfloat16)
        fitted = dot32(coef, basis_t_ref[...]) * weight_ref[i]
        group = ids_ref[item * batch + i]
        total_ref[group, :size] += fringe_ref[i].astype(jnp.float32) - fitted
        total_ref[group, size:] += jnp.ones_like(total_ref[group, size:])

    @pl.when(item == pl.num_programs(0) - 1)
    def _():
        out_ref[...] = total_ref[...].astype(jnp.bfloat16)


def newton_scales(low, high):
    scales = []
    value = (high + low) / (high - low)
    while True:
        doubled = 2.0 * value * value
        scales.append(doubled / (doubled - 1.0))
        value = doubled - 1.0
        if value > 1e6:
            return scales


def full(shape):
    return pl.BlockSpec(shape, lambda i, *rest: (0,) * len(shape))


def lead(shape):
    return pl.BlockSpec(shape, lambda i, *rest: (i,) + (0,) * (len(shape) - 1))


def second(shape):
    return pl.BlockSpec(shape, lambda i, *rest: (0, i) + (0,) * (len(shape) - 2))


def per_device_general(vis, flags, band, group_id):
    items, chan, _, length = vis.shape
    both = 2 * length
    shards = lax.axis_size("freq")
    owners = lax.axis_size("bl")
    groups = GPO * owners
    time_local = length // shards
    rows = 2 * time_local
    pair = 2 if items % 2 == 0 else 1
    chunks = 2 if rows % 32 == 0 else 1
    rows //= chunks
    size = both // chunks
    bf16, f32 = jnp.bfloat16, jnp.float32

    table = fourier_tables(length)
    forward = jnp.asarray(table)
    inverse_t = forward
    if chunks == 1:
        inverse_t = table.reshape(2, shards, time_local, both)
        inverse_t = jnp.asarray(np.transpose(inverse_t, (1, 0, 2, 3)).reshape(both, both))
    response = band_response(band, length, NBAND).reshape(items, 1, both)
    basis = make_basis(CH, DELAYS)
    basis_t = jnp.asarray(basis.T.copy())
    basis = jnp.asarray(basis)
    basis_local = lax.dynamic_slice_in_dim(basis, lax.axis_index("freq") * chan, chan, 0)
    weight = 1.0 - flags.astype(f32)
    weight_rows = weight.reshape(items, 1, chan)
    weight_half = weight.astype(bf16)
    if shards <= 8:
        pieces = [weight_half] + [
            lax.ppermute(weight_half, "freq", [(d, (d - j) % shards) for d in range(shards)])
            for j in range(1, shards)
        ]
        doubled = jnp.concatenate(pieces + pieces, axis=1)
        offset = (shards - lax.axis_index("freq")) % shards * chan
        weight_full = lax.dynamic_slice_in_dim(doubled, offset, CH, 1)
    else:
        weight_full = lax.all_gather(weight_half, "freq", axis=1, tiled=True)
        response, weight_full = lax.optimization_barrier((response, weight_full))
    weight_full = weight_full.reshape(items, 1, CH)

    fringe, projected = pl.pallas_call(
        functools.partial(filter_kernel, shards, chunks),
        grid=(items // pair,),
        in_specs=[
            lead((pair, chan, 2, length)), full((both, both)), full((both, both)),
            lead((pair, 1, both)), lead((pair, 1, chan)), full((chan, DELAYS)),
        ],
        out_specs=[lead((pair, both, chan)), second((shards, pair, chunks, rows, DELAYS))],
        out_shape=[
            jax.ShapeDtypeStruct((items, both, chan), bf16),
            jax.ShapeDtypeStruct((shards, items, chunks, rows, DELAYS), bf16),
        ],
        compiler_params=pltpu.CompilerParams(vmem_limit_bytes=BIG),
        cost_estimate=pl.CostEstimate(
            flops=4 * items * chan * both * both, bytes_accessed=4 * items * chan * both,
            transcendentals=0,
        ),
    )(vis, forward, inverse_t, response, weight_rows, basis_local)

    projected, weight_full = lax.optimization_barrier((projected, weight_full))
    ridge = CH / 64.0
    high = ridge + 1.05 * CH
    batch = 4 if items % 4 == 0 else 1
    inverse = pl.pallas_call(
        functools.partial(
            inverse_kernel, batch, ridge, newton_scales(ridge, high), 2.0 / (ridge + high)
        ),
        grid=(items // batch,),
        in_specs=[lead((batch, 1, CH)), full((CH, DELAYS)), full((DELAYS, CH))],
        out_specs=lead((batch, DELAYS, DELAYS)),
        out_shape=jax.ShapeDtypeStruct((items, DELAYS, DELAYS), f32),
        compiler_params=pltpu.CompilerParams(vmem_limit_bytes=BIG),
        cost_estimate=pl.CostEstimate(
            flops=20_000_000_000, bytes_accessed=4 * items * DELAYS * DELAYS, transcendentals=0
        ),
    )(weight_full, basis, basis_t)

    received = lax.all_to_all(projected, "freq", split_axis=0, concat_axis=0, tiled=True)
    coefficients = pl.pallas_call(
        functools.partial(solve_kernel, batch),
        grid=(items // batch,),
        in_specs=[
            second((shards, batch, chunks, rows, DELAYS)), lead((batch, DELAYS, DELAYS)),
        ],
        out_specs=[second((1, batch, rows, DELAYS))] * chunks,
        out_shape=[jax.ShapeDtypeStruct((1, items, rows, DELAYS), bf16)] * chunks,
        compiler_params=pltpu.CompilerParams(vmem_limit_bytes=BIG),
    )(received, inverse)
    basis_local_t = basis_local.T
    tall = size + 16

    def clean(h, gathered):
        return pl.pallas_call(
            clean_kernel,
            grid_spec=pltpu.PrefetchScalarGridSpec(
                num_scalar_prefetch=1,
                grid=(items // batch,),
                in_specs=[
                    pl.BlockSpec((batch, size, chan), lambda i, ids: (i, h, 0)),
                    pl.BlockSpec((1, shards, batch, rows, DELAYS), lambda i, ids: (0, 0, i, 0, 0)),
                    full((DELAYS, chan)),
                    lead((batch, 1, chan)),
                ],
                out_specs=full((groups, tall, chan)),
                scratch_shapes=[pltpu.VMEM((groups, tall, chan), f32)],
            ),
            out_shape=jax.ShapeDtypeStruct((groups, tall, chan), bf16),
            compiler_params=pltpu.CompilerParams(vmem_limit_bytes=58 * 1024 * 1024),
            cost_estimate=pl.CostEstimate(
                flops=2_000_000_000, bytes_accessed=4 * items * size * chan, transcendentals=0
            ),
        )(group_id, fringe, gathered, basis_local_t, weight_rows)

    pieces = []
    for h in range(chunks):
        part = coefficients[h]
        if h:
            part, sums = lax.optimization_barrier((part, sums))
        sums = clean(h, gather_chain(part, shards, 1, h))
        if h:
            sums, pieces[-1] = lax.optimization_barrier((sums, pieces[-1]))
        arrived = lax.all_to_all(sums, "bl", split_axis=0, concat_axis=0, tiled=True)
        total = jnp.sum(arrived.reshape(owners, GPO, tall, chan).astype(f32), 0)
        counts = jnp.maximum(total[:, size:size + 1, :1], 1.0)
        mean = (total[:, :size] / counts).astype(bf16).reshape(GPO, shards, rows, chan)
        pieces.append(jnp.transpose(mean, (1, 0, 2, 3)))
    if shards > 8:
        swapped = [
            lax.all_to_all(piece, "freq", split_axis=0, concat_axis=0, tiled=True)
            for piece in pieces
        ]
        swapped = [jnp.concatenate(list(piece), axis=-1) for piece in swapped]
    else:
        me = lax.axis_index("freq")
        swapped = []
        for piece in pieces:
            parts = [lax.dynamic_index_in_dim(piece, me, 0, keepdims=False)]
            for j in range(1, shards):
                out = lax.dynamic_index_in_dim(piece, (me + shards - j) % shards, 0, keepdims=False)
                parts.append(
                    lax.ppermute(out, "freq", [(d, (d - j) % shards) for d in range(shards)])
                )
            doubled = jnp.concatenate(parts + parts, axis=-1)
            offset = (shards - me) % shards * chan
            swapped.append(lax.dynamic_slice_in_dim(doubled, offset, CH, 2))
    averaged = [piece.reshape(GPO, 2 // chunks, time_local, CH) for piece in swapped]
    return jnp.concatenate(averaged, 1)


MESH = pl.DeviceIdType.MESH
RANK = 48


def filter_tables(length, shards):
    sample_index = np.arange(length)
    phase_index = sample_index[:, None] * sample_index[None, :] % length
    angles = phase_index.astype(np.float32) * np.float32(2.0 * math.pi / length)
    cosine = np.cos(angles).astype(jnp.bfloat16).astype(np.float64)
    sine = np.sin(angles).astype(jnp.bfloat16).astype(np.float64)
    signed = (sample_index - length * (sample_index >= length // 2)).astype(np.float64)
    tables = []
    for band in range(NBAND):
        center = (band - (NBAND - 1) / 2.0) * (length / (4.0 * NBAND))
        ratio = (signed - center) / (length / 32.0)
        response = (0.15 + 0.85 / (1.0 + ratio**4)) / length
        even = (cosine * response) @ cosine + (sine * response) @ sine
        odd = (cosine * response) @ sine - (sine * response) @ cosine
        whole = np.concatenate(
            [np.concatenate([even, odd], 1), np.concatenate([-odd, even], 1)], 0
        )
        tables.append(whole)
    tables = np.stack(tables).reshape(NBAND, 2 * length, 2, shards, length // shards)
    tables = np.transpose(tables, (3, 0, 1, 2, 4))
    return tables.reshape(shards, NBAND, 2 * length, 2 * length // shards).astype(jnp.bfloat16)


def factored_basis(channels, modes, shards):
    size = channels // shards
    channel_index = np.arange(channels)
    order_index = np.arange(modes)
    phase = (order_index[None, :] * (2 * channel_index[:, None] + 1) % (4 * channels)).astype(
        np.longdouble
    )
    exact = np.cos(phase * (np.longdouble(np.pi) / (2 * channels)))
    fronts, backs = [], []
    for z in range(shards):
        block = exact[z * size:(z + 1) * size]
        rest = block.copy()
        columns = []
        for _ in range(RANK):
            norms = (rest * rest).sum(0)
            best = int(np.argmax(norms))
            column = rest[:, best] / np.sqrt(norms[best])
            for other in columns:
                column = column - other * (other * column).sum()
            column = column / np.sqrt((column * column).sum())
            columns.append(column)
            rest = rest - column[:, None] * (column[:, None] * rest).sum(0)[None]
        front = np.stack(columns)
        fronts.append(front)
        backs.append(np.stack([(row[:, None] * block).sum(0) for row in front]))
    fronts = np.stack(fronts).astype(np.float32)
    spread = np.zeros((shards, 2, RANK, size, 2), np.float32)
    for r in range(2):
        spread[:, r, :, :, r] = fronts
    fronts = spread.reshape(shards, 2 * RANK, 2 * size).astype(jnp.bfloat16)
    backs = np.concatenate(backs).astype(np.float32).astype(jnp.bfloat16)
    return fronts, backs.T.copy()


def dot_nt(left, right):
    return lax.dot_general(left, right, NT, preferred_element_type=jnp.float32)


def main_kernel(ridge, scales, start_scale, ids, bands, vis_hbm, flags_ref, m_hbm, front_hbm,
                back_ref, basis_hbm, basis_t_hbm, out_ref,
                vis_v, m_v, front_v, basis_v, basis_t_v, sep_a, sep_b, pick_a, pick_b, weight_v, half_v, spread_v, turned_v, sums_a, sums_b,
                pair_send_a, pair_send_b, pair_recv_a, pair_recv_b, cross_send_a, cross_send_b,
                cross_recv_a, cross_recv_b, far_send_a, far_send_b, far_recv_a, far_recv_b,
                y_send, y_recv, w_recv, wide, inv_v, coef_v, coef_send, coef_recv,
                code_tmp, code_send, code_recv, left_v, right_v, fit_v,
                prev_s, last_s, next_s, slot_s, local_sem, send_sem, recv_sem):
    f32, bf16 = jnp.float32, jnp.bfloat16
    items, chan = vis_v.shape[0], vis_v.shape[1]
    length = vis_v.shape[3]
    rt = m_v.shape[3]
    modes = basis_v.shape[1]
    me_b, me_f = lax.axis_index("bl"), lax.axis_index("freq")
    me_x, me_c = me_b // 2, lax.rem(me_b, 2)
    far = [lax.rem(me_f + 2, 4), 3 - me_f, me_f + 1 - 2 * lax.rem(me_f, 2), me_f]
    sibling = me_b + 1 - 2 * me_c
    across = lax.rem(me_b + 2, 4)
    diagonal = 3 - me_b
    owners = [me_b, sibling, across, diagonal]
    sums = (sums_a, sums_b)
    pair_send, pair_recv = (pair_send_a, pair_send_b), (pair_recv_a, pair_recv_b)
    cross_send, cross_recv = (cross_send_a, cross_send_b), (cross_recv_a, cross_recv_b)
    far_send, far_recv = (far_send_a, far_send_b), (far_recv_a, far_recv_b)
    spans = [(0, sums_a.shape[1]), (sums_a.shape[1], sums_b.shape[1])]
    chunk = items // 4

    def load(i):
        return pltpu.make_async_copy(
            vis_hbm.at[pl.ds(i * chunk, chunk)], vis_v.at[pl.ds(i * chunk, chunk)],
            local_sem.at[i],
        )

    tables = [
        pltpu.make_async_copy(m_hbm.at[far[j]], m_v.at[j], local_sem.at[4 + j])
        for j in range(4)
    ]
    bases = [
        pltpu.make_async_copy(basis_hbm, basis_v, local_sem.at[8]),
        pltpu.make_async_copy(basis_t_hbm, basis_t_v, local_sem.at[9]),
    ]
    front = pltpu.make_async_copy(front_hbm.at[me_f], front_v, local_sem.at[10])
    for copy in [load(0), front] + tables + [load(i) for i in range(1, 4)] + bases:
        copy.start()

    barrier = pltpu.get_barrier_semaphore()
    for j in range(3):
        pl.semaphore_signal(barrier, inc=1, device_id={"freq": far[j]}, device_id_type=MESH)
        pl.semaphore_signal(barrier, inc=1, device_id={"bl": owners[j + 1]}, device_id_type=MESH)

    weight_v[...] = 1.0 - flags_ref[...].astype(f32)
    half_v[...] = weight_v[...].astype(bf16)
    repeat = (
        lax.broadcasted_iota(jnp.int32, (chan, 2 * chan), 1) // 2
        == lax.broadcasted_iota(jnp.int32, (chan, 2 * chan), 0)
    ).astype(f32)
    spread_v[...] = dot32(half_v[...], repeat.astype(bf16))
    padded = jnp.concatenate([weight_v[...], jnp.zeros((128 - items, chan), f32)], 0)
    turned_v[...] = padded.T.astype(bf16)
    for total in sums:
        total[0] = jnp.zeros_like(total[0])
    group = [ids[b] for b in range(items)]
    for b in range(items):
        before, after = jnp.int32(0), jnp.int32(items)
        for other in range(b):
            before = jnp.where(group[other] == group[b], other + 1, before)
        for other in reversed(range(b + 1, items)):
            after = jnp.where(group[other] // GPO == group[b] // GPO, other, after)
        prev_s[b] = before
        next_s[b] = after
    next_s[items] = jnp.int32(items)
    for g in range(4 * GPO):
        end = jnp.int32(0)
        for b in range(items):
            end = jnp.where(group[b] == g, b + 1, end)
        last_s[g] = end
    for o in range(4):
        place = jnp.int32(items)
        for b in reversed(range(items)):
            place = jnp.where(group[b] // GPO == o, b, place)
        for step in range(CAP):
            slot_s[o * CAP + step] = place
            place = next_s[place]

    pl.semaphore_wait(barrier, 6)

    pending = []

    def remote(index, source, target, axis, place):
        return pltpu.make_async_remote_copy(
            src_ref=source, dst_ref=target, send_sem=send_sem.at[index],
            recv_sem=recv_sem.at[index], device_id={axis: place}, device_id_type=MESH,
        )

    def send(index, source, target, axis, place):
        copy = remote(index, source, target, axis, place)
        copy.start()
        pending.append(copy)
        return copy

    def y_copy(j, c):
        part = pl.ds(c * chunk, chunk)
        return remote(
            31 + 4 * j + c, y_send.at[j, part], y_recv.at[me_f, part], "freq", far[j]
        )

    w_copies = [send(j, half_v, w_recv.at[me_f], "freq", far[j]) for j in range(3)]

    def separate(b, span, target, pick):
        at, size = span
        values = vis_v[b, at:at + size].astype(f32).reshape(2 * size, length)
        for h in range(length // 128):
            pick[h, :2 * size] = values[:, h * 128:(h + 1) * 128]
        chosen = (lax.broadcasted_iota(jnp.int32, (128, 128), 0) == b).astype(f32).astype(bf16)
        mask = dot32(turned_v[at:at + size], chosen)
        for r in range(2):
            for h in range(length // 128):
                place = r * length + h * 128
                target[:size, place:place + 128] = (
                    pick[h, pl.ds(r, size, stride=2), :] * mask
                ).astype(bf16)

    def table_of(b):
        return jnp.concatenate([m_v[j, bands[b]] for j in range(4)], 1)

    def project(b, target, at):
        rows = vis_v[b].reshape(2 * chan, length)
        picked = front_v[...] * spread_v[pl.ds(b, 1), :].astype(bf16)
        raw = dot32(picked, rows).astype(bf16)
        target[at:at + RANK, :length] = raw[:RANK]
        target[at:at + RANK, length:] = raw[RANK:]

    def filter_one(b, q, source):
        size = spans[q][1]
        rows = size + RANK if q == 0 else size
        fringe = dot32(source[:rows], table_of(b))
        sums[q][b + 1] = sums[q][prev_s[b]] + fringe[:size]
        if q == 0:
            y = fringe[size:].astype(bf16)
            for j in range(3):
                y_send[j, b] = y[:, j * rt:(j + 1) * rt]
            y_recv[me_f, b] = y[:, 3 * rt:]

    for table in tables:
        table.wait()
    front.wait()

    def project_chunk(c, carry):
        load(c).wait()
        for i in range(chunk):
            target, pick = ((sep_a, pick_a), (sep_b, pick_b))[i % 2]
            separate(c * chunk + i, spans[0], target, pick)
            project(c * chunk + i, target, spans[0][1])
            filter_one(c * chunk + i, 0, target)
        for j in range(3):
            y_copy(j, c).start()
        return carry

    lax.fori_loop(0, 4, project_chunk, 0)

    pair_copies, cross_copies, far_copies = [[], []], [[], []], []

    def filter_span(q, first, last):
        def filter_pair(t, carry):
            separate(2 * t + 1, spans[q], sep_b, pick_b)
            filter_one(2 * t, q, sep_a)
            separate(jnp.minimum(2 * t + 2, items - 1), spans[q], sep_a, pick_a)
            filter_one(2 * t + 1, q, sep_b)
            return carry

        lax.fori_loop(first, last, filter_pair, 0)

    def pair_start(q):
        for j in range(4):
            for x in range(2):
                for l in range(GPO):
                    g = GPO * (2 * x + 1 - me_c) + l
                    part = sums[q][last_s[g], :, j * rt:(j + 1) * rt]
                    pair_send[q][j, GPO * x + l] = part.astype(bf16)
            pair_copies[q].append(
                send(3 + 4 * q + j, pair_send[q].at[j], pair_recv[q].at[j], "bl", sibling)
            )

    def pair_stage(q):
        for j in range(4):
            pair_copies[q][j].wait_recv()
            for l in range(GPO):
                mine = sums[q][last_s[GPO * across + l], :, j * rt:(j + 1) * rt]
                other = pair_recv[q][j, GPO * (1 - me_x) + l].astype(f32)
                cross_send[q][j, l] = (mine + other).astype(bf16)
            cross_copies[q].append(
                send(11 + 4 * q + j, cross_send[q].at[j], cross_recv[q].at[j], "bl", across)
            )

    def cross_stage(q, j):
        cross_copies[q][j].wait_recv()
        for l in range(GPO):
            total = sums[q][last_s[GPO * me_b + l], :, j * rt:(j + 1) * rt]
            total = total + pair_recv[q][j, GPO * me_x + l].astype(f32)
            total = (total + cross_recv[q][j, l].astype(f32)).astype(bf16)
            if j < 3:
                far_send[q][j, l] = total
            else:
                far_recv[q][me_f, l] = total
        if j < 3:
            far_copies.append(
                send(19 + 3 * q + j, far_send[q].at[j], far_recv[q].at[me_f], "freq", far[j])
            )

    pair_start(0)
    separate(0, spans[1], sep_a, pick_a)
    filter_span(1, 0, 2)
    pair_stage(0)
    filter_span(1, 2, items // 2)
    pair_start(1)

    for copy in w_copies:
        copy.wait_recv()
    w_recv[me_f] = half_v[...]
    for z in range(4):
        wide[:items, z * chan:(z + 1) * chan] = w_recv[z].astype(f32)
    wide[items:, :] = jnp.zeros_like(wide[items:, :])

    half = wide.shape[1] // 2
    code_copies = []
    for k in range(4):
        for s in range(CAP):
            place = slot_s[owners[k] * CAP + s]
            local = lax.rem(ids[jnp.minimum(place, items - 1)], GPO) + 1
            code = jnp.where(place < items, local, 0).astype(f32)
            row = wide[pl.ds(place, 1), :] * code
            for h in range(2):
                code_tmp[h * CAP + s:h * CAP + s + 1, :half] = row[:, h * half:(h + 1) * half]
                code_tmp[h * CAP + s:h * CAP + s + 1, half:] = (
                    jnp.zeros((1, code_tmp.shape[1] - half), f32) + code
                )
        if k == 0:
            code_recv[me_b] = code_tmp[...].astype(bf16)
        else:
            code_send[k - 1] = code_tmp[...].astype(bf16)
            code_copies.append(
                send(24 + k, code_send.at[k - 1], code_recv.at[me_b], "bl", owners[k])
            )

    for copy in bases:
        copy.wait()
    eye = (
        lax.broadcasted_iota(jnp.int32, (modes, modes), 0)
        == lax.broadcasted_iota(jnp.int32, (modes, modes), 1)
    ).astype(f32)
    batch = 4

    def invert(step, carry):
        normals = []
        for i in range(batch):
            weight = wide[pl.ds(step * batch + i, 1), :].astype(bf16)
            normals.append(dot32(basis_t_v[...] * weight, basis_v[...]) + ridge * eye)
        guess = [
            scales[0] * (2.0 * start_scale * eye - start_scale * start_scale * normal)
            for normal in normals
        ]
        normals = [halves(normal) for normal in normals]
        for turn, scale in enumerate(scales[1:]):
            parts = [halves(value) for value in guess]
            if turn + 3 < len(scales) - 1:
                product = [dot32(n[0], g[0]) for n, g in zip(normals, parts)]
            else:
                product = [dot_split(n, g) for n, g in zip(normals, parts)]
            error = [(eye - value).astype(bf16) for value in product]
            guess = [
                scale * (value + dot32(g[0], e)) for value, g, e in zip(guess, parts, error)
            ]
        for i in range(batch):
            inv_v[step * batch + i] = guess[i]
        return carry

    for j in range(4):
        cross_stage(0, j)
    pair_stage(1)
    for j in range(4):
        lax.fori_loop(j, j + 1, invert, 0)
        if j < 3:
            cross_stage(1, j)

    def solve(p, carry):
        values = y_recv[:, p].reshape(-1, rt)
        projected = dot32(back_ref[...], values).T
        coef_v[p] = dot_split(halves(projected), halves(inv_v[p])).astype(bf16)
        return carry

    for c in range(4):
        for j in range(3):
            y_copy(j, c).wait_recv()
        lax.fori_loop(c * chunk, (c + 1) * chunk, solve, 0, unroll=4)
    coef_v[items] = jnp.zeros_like(coef_v[items])
    coef_copies = []
    for k in (2, 3, 1, 0):
        for s in range(CAP):
            value = coef_v[slot_s[owners[k] * CAP + s]]
            if k == 0:
                coef_recv[me_b, s] = value
            else:
                coef_send[k - 1, s] = value
        if k > 0:
            coef_copies.append(
                send(27 + k, coef_send.at[k - 1], coef_recv.at[me_b], "bl", owners[k])
            )

    cross_stage(1, 3)
    counts = [jnp.zeros((1, 128), f32) for _ in range(GPO)]
    for k in range(4):
        if k > 0:
            code_copies[k - 1].wait_recv()
            coef_copies[{1: 2, 2: 0, 3: 1}[k]].wait_recv()
        place = owners[k]
        codes = code_recv[place].astype(f32)
        for s in range(CAP):
            value = coef_recv[place, s].astype(f32)
            for l in range(GPO):
                match = (codes[s:s + 1, half:half + 128] == 1.0 + l).astype(f32)
                counts[l] = counts[l] + match
                left_v[l * rt:(l + 1) * rt, s * modes:(s + 1) * modes] = (value * match).astype(
                    bf16
                )
        for h in range(2):
            for s in range(CAP):
                row = codes[h * CAP + s:h * CAP + s + 1, :half]
                weight = (row > 0.0).astype(f32).astype(bf16)
                right_v[s * modes:(s + 1) * modes, :] = (
                    basis_t_v[:, h * half:(h + 1) * half] * weight
                )
            fitted = dot32(left_v[...], right_v[...])
            if k == 0:
                fit_v[:, h * half:(h + 1) * half] = fitted
            else:
                fit_v[:, h * half:(h + 1) * half] = fit_v[:, h * half:(h + 1) * half] + fitted

    for copy in far_copies:
        copy.wait_recv()
    for l in range(GPO):
        share = 1.0 / jnp.maximum(counts[l][:, :1], 1.0)
        for z in range(4):
            for q, (low, size) in enumerate(spans):
                at = z * chan + low
                rest = far_recv[q][z, l].astype(f32).T
                rest = rest - fit_v[l * rt:(l + 1) * rt, at:at + size]
                out_ref[l, :, at:at + size] = (rest * share).astype(bf16)
    for c in range(4):
        for j in range(3):
            y_copy(j, c).wait_send()
    for copy in pending:
        copy.wait_send()


def per_device_fused(vis, flags, band, group_id):
    items, chan, _, length = vis.shape
    shards = 4
    f32, bf16 = jnp.float32, jnp.bfloat16
    rt = 2 * length // shards
    channels = chan * shards
    smem = pl.BlockSpec(memory_space=pltpu.SMEM)
    vmem = pl.BlockSpec(memory_space=pltpu.VMEM)
    hbm = pl.BlockSpec(memory_space=pltpu.HBM)
    table = jnp.asarray(filter_tables(length, shards))
    fronts, backs = factored_basis(channels, DELAYS, shards)
    basis = make_basis(channels, DELAYS)
    ridge = channels / 64.0
    high = ridge + 1.05 * channels
    half = channels // 2
    narrow = 128
    out = pl.pallas_call(
        functools.partial(main_kernel, ridge, newton_scales(ridge, high), 2.0 / (ridge + high)),
        in_specs=[smem, smem, hbm, vmem, hbm, hbm, vmem, hbm, hbm],
        out_specs=vmem,
        out_shape=jax.ShapeDtypeStruct((GPO, rt, channels), bf16),
        scratch_shapes=[
            pltpu.VMEM(vis.shape, bf16),
            pltpu.VMEM((shards, NBAND, 2 * length, rt), bf16),
            pltpu.VMEM((2 * RANK, 2 * chan), bf16),
            pltpu.VMEM((channels, DELAYS), bf16),
            pltpu.VMEM((DELAYS, channels), bf16),
            pltpu.VMEM((chan, 2 * length), bf16),
            pltpu.VMEM((chan, 2 * length), bf16),
            pltpu.VMEM((length // 128, 2 * chan, 128), f32),
            pltpu.VMEM((length // 128, 2 * chan, 128), f32),
            pltpu.VMEM((items, chan), f32),
            pltpu.VMEM((items, chan), bf16),
            pltpu.VMEM((items, 2 * chan), f32),
            pltpu.VMEM((chan, 128), bf16),
            pltpu.VMEM((items + 1, narrow, 2 * length), f32),
            pltpu.VMEM((items + 1, chan - narrow, 2 * length), f32),
        ] + [
            pltpu.VMEM(lead_shape + (size, rt), bf16)
            for lead_shape in ((4, 2 * GPO), (4, 2 * GPO), (4, GPO), (4, GPO), (3, GPO), (shards, GPO))
            for size in (narrow, chan - narrow)
        ] + [
            pltpu.VMEM((3, items, RANK, rt), bf16),
            pltpu.VMEM((shards, items, RANK, rt), bf16),
            pltpu.VMEM((shards, items, chan), bf16),
            pltpu.VMEM((items + 8, channels), f32),
            pltpu.VMEM((items, DELAYS, DELAYS), f32),
            pltpu.VMEM((items + 1, rt, DELAYS), bf16),
            pltpu.VMEM((3, CAP, rt, DELAYS), bf16),
            pltpu.VMEM((4, CAP, rt, DELAYS), bf16),
            pltpu.VMEM((2 * CAP, half + 128), f32),
            pltpu.VMEM((3, 2 * CAP, half + 128), bf16),
            pltpu.VMEM((4, 2 * CAP, half + 128), bf16),
            pltpu.VMEM((GPO * rt, CAP * DELAYS), bf16),
            pltpu.VMEM((CAP * DELAYS, half), bf16),
            pltpu.VMEM((GPO * rt, channels), f32),
            pltpu.SMEM((items,), jnp.int32),
            pltpu.SMEM((4 * GPO,), jnp.int32),
            pltpu.SMEM((items + 1,), jnp.int32),
            pltpu.SMEM((4 * CAP,), jnp.int32),
            pltpu.SemaphoreType.DMA((11,)),
            pltpu.SemaphoreType.DMA((43,)),
            pltpu.SemaphoreType.DMA((43,)),
        ],
        compiler_params=pltpu.CompilerParams(
            collective_id=0, has_side_effects=True, vmem_limit_bytes=56 * 1024 * 1024
        ),
        cost_estimate=pl.CostEstimate(
            flops=10_000_000_000, bytes_accessed=4 * vis.size, transcendentals=0
        ),
    )(
        group_id, band, vis, flags, table, jnp.asarray(fronts), jnp.asarray(backs),
        jnp.asarray(basis), jnp.asarray(basis.T.copy()),
    )
    return out.reshape(GPO, 2, length // shards, channels)


def per_device(vis, flags, band, group_id):
    items, chan, _, length = vis.shape
    fits = (
        lax.axis_size("freq") == 4 and lax.axis_size("bl") == 4 and items == 16
        and chan % 128 == 0 and chan > 128 and length == 256
    )
    return (per_device_fused if fits else per_device_general)(vis, flags, band, group_id)


def solution(mesh):
    in_specs = (P("bl", "freq", None, "win"), P("bl", "freq"), P("bl"), P("bl"))
    out_specs = P("bl", None, ("win", "freq"), None)
    return jax.shard_map(
        per_device, mesh=mesh, in_specs=in_specs, out_specs=out_specs, check_vma=False
    )
```

```python
import functools
import math

import jax
import jax.numpy as jnp
import numpy as np
from jax import lax
from jax.experimental import pallas as pl
from jax.experimental.pallas import tpu as pltpu
from jax.sharding import PartitionSpec as P

CH = 1536
DELAYS = 128
NBAND = 8
GPO = 2
CAP = 8


def fourier_tables(length):
    sample_index = np.arange(length, dtype=np.int32)
    phase_index = sample_index[:, None] * sample_index[None, :] % length
    angles = phase_index.astype(np.float32) * np.float32(2.0 * math.pi / length)
    cosine = np.cos(angles)
    sine_table = np.sin(angles)
    forward = np.concatenate(
        [np.concatenate([cosine, -sine_table], 1), np.concatenate([sine_table, cosine], 1)], 0
    )
    return forward.astype(jnp.bfloat16)


def band_response(band, length, band_count):
    mode_index = jnp.arange(length, dtype=jnp.int32)
    signed_modes = (mode_index - length * (mode_index >= length // 2).astype(jnp.int32)).astype(
        jnp.float32
    )
    center = (band.astype(jnp.float32) - (band_count - 1) / 2.0) * (length / (4.0 * band_count))
    band_width = length / 32.0
    offset_ratio = (signed_modes[None, :] - center[:, None]) / band_width
    single = (0.15 + 0.85 / (1.0 + offset_ratio**4)) / length
    return jnp.concatenate([single, single], 1)


def make_basis(channels, modes):
    channel_index = np.arange(channels, dtype=np.int32)
    order_index = np.arange(modes, dtype=np.int32)
    phase_index = order_index[None, :] * (2 * channel_index[:, None] + 1) % (4 * channels)
    return np.cos(phase_index.astype(np.float32) * np.float32(math.pi / (2 * channels))).astype(
        jnp.bfloat16
    )


NT = (((1,), (1,)), ((), ()))
BIG = 48 * 1024 * 1024


def dot32(left, right):
    return jnp.dot(left, right, preferred_element_type=jnp.float32)


def halves(value):
    high = value.astype(jnp.bfloat16)
    return high, (value - high.astype(jnp.float32)).astype(jnp.bfloat16)


def dot_split(left, right):
    left_high, left_low = left
    right_high, right_low = right
    return dot32(left_high, right_high) + (
        dot32(left_high, right_low) + dot32(left_low, right_high)
    )


def filter_kernel(shards, chunks, vis_ref, fwd_ref, inv_ref, resp_ref, weight_ref, basis_ref,
                  fringe_ref, proj_ref):
    batch, half = vis_ref.shape[0], vis_ref.shape[3]
    spectra = [
        dot32(vis_ref[i, :, 0, :], fwd_ref[:half]) + dot32(vis_ref[i, :, 1, :], fwd_ref[half:])
        for i in range(batch)
    ]
    spectra = [(spectra[i] * resp_ref[i]).astype(jnp.bfloat16) for i in range(batch)]
    for i in range(batch):
        fringe = lax.dot_general(inv_ref[...], spectra[i], NT, preferred_element_type=jnp.float32)
        fringe = (fringe * weight_ref[i]).astype(jnp.bfloat16)
        fringe_ref[i] = fringe
        projected = dot32(fringe, basis_ref[...])
        size = projected.shape[0] // chunks
        for h in range(chunks):
            piece = projected[h * size:(h + 1) * size].reshape(shards, -1, projected.shape[1])
            proj_ref[:, i, h] = piece.astype(jnp.bfloat16)


def inverse_kernel(batch, ridge, scales, start, weight_ref, basis_ref, basis_t_ref, out_ref):
    modes = out_ref.shape[1]
    eye = (
        lax.broadcasted_iota(jnp.int32, (modes, modes), 0)
        == lax.broadcasted_iota(jnp.int32, (modes, modes), 1)
    ).astype(jnp.float32)
    normals = [
        dot32(basis_t_ref[...] * weight_ref[i], basis_ref[...]) + ridge * eye for i in range(batch)
    ]
    first = scales[0]
    guess = [first * (2.0 * start * eye - start * start * normal) for normal in normals]
    normals = [halves(normal) for normal in normals]
    for scale in scales[1:]:
        guess_parts = [halves(value) for value in guess]
        product = [dot_split(n, g) for n, g in zip(normals, guess_parts)]
        change = [halves(2.0 * eye - value) for value in product]
        guess = [scale * dot_split(g, c) for g, c in zip(guess_parts, change)]
    for i in range(batch):
        out_ref[i] = guess[i]


def solve_kernel(batch, recv_ref, inverse_ref, *out_refs):
    for i in range(batch):
        inverse = halves(inverse_ref[i])
        for h, out_ref in enumerate(out_refs):
            total = jnp.sum(recv_ref[:, i, h].astype(jnp.float32), axis=0)
            out_ref[0, i] = dot_split(halves(total), inverse).astype(jnp.bfloat16)


def chain_kernel(shards, chunks, own_ref, out_ref, send_sem, recv_sem):
    me = lax.axis_index("freq")
    has_right, has_left = me < shards - 1, me > 0
    barrier = pltpu.get_barrier_semaphore()

    def greet(has, step):
        @pl.when(has)
        def _():
            pl.semaphore_signal(
                barrier, inc=1, device_id={"freq": me + step},
                device_id_type=pl.DeviceIdType.MESH,
            )

    greet(has_right, 1)
    greet(has_left, -1)
    pl.semaphore_wait(barrier, has_right.astype(jnp.int32) + has_left.astype(jnp.int32))

    def copy(way, h, hop, step):
        source = me - step * hop
        start = own_ref.at[h] if hop == 0 else out_ref.at[h, source]
        return pltpu.make_async_remote_copy(
            src_ref=start,
            dst_ref=out_ref.at[h, source],
            send_sem=send_sem.at[way, h, hop],
            recv_sem=recv_sem.at[way, h, hop],
            device_id={"freq": me + step},
            device_id_type=pl.DeviceIdType.MESH,
        )

    def arrival(way, h, hop, step):
        source = me - step * (hop + 1)
        return pltpu.make_async_remote_copy(
            src_ref=own_ref.at[h],
            dst_ref=out_ref.at[h, source],
            send_sem=send_sem.at[way, h, hop],
            recv_sem=recv_sem.at[way, h, hop],
            device_id={"freq": me - step},
            device_id_type=pl.DeviceIdType.MESH,
        )

    ways = ((0, 1, has_right), (1, -1, has_left))
    for hop in range(shards):
        for h in range(chunks):
            for way, step, has in ways:
                source = me - step * hop
                held = jnp.logical_and(source >= 0, source <= shards - 1)
                if hop > 0:
                    @pl.when(held)
                    def _():
                        arrival(way, h, hop - 1, step).wait_recv()
                if hop < shards - 1:
                    @pl.when(jnp.logical_and(held, has))
                    def _():
                        copy(way, h, hop, step).start()
        if hop == 0:
            for h in range(chunks):
                out_ref[h, me] = own_ref[h]
    for hop in range(shards - 1):
        for h in range(chunks):
            for way, step, has in ways:
                source = me - step * hop
                held = jnp.logical_and(source >= 0, source <= shards - 1)

                @pl.when(jnp.logical_and(held, has))
                def _():
                    copy(way, h, hop, step).wait_send()


def gather_chain(part, shards, chunks, call):
    if shards > 8:
        return jnp.stack([lax.all_gather(part[h], "freq") for h in range(chunks)])
    hops = max(shards - 1, 1)
    return pl.pallas_call(
        functools.partial(chain_kernel, shards, chunks),
        in_specs=[pl.BlockSpec(memory_space=pltpu.VMEM)],
        out_specs=pl.BlockSpec(memory_space=pltpu.VMEM),
        out_shape=jax.ShapeDtypeStruct((chunks, shards) + part.shape[1:], part.dtype),
        scratch_shapes=[
            pltpu.SemaphoreType.DMA((2, chunks, hops)),
            pltpu.SemaphoreType.DMA((2, chunks, hops)),
        ],
        compiler_params=pltpu.CompilerParams(
            collective_id=call, has_side_effects=True, vmem_limit_bytes=58 * 1024 * 1024
        ),
        cost_estimate=pl.CostEstimate(
            flops=20_000_000_000, bytes_accessed=2 * shards * part.size, transcendentals=0
        ),
    )(part)


def clean_kernel(ids_ref, fringe_ref, coef_ref, basis_t_ref, weight_ref, out_ref, total_ref):
    item = pl.program_id(0)

    @pl.when(item == 0)
    def _():
        total_ref[...] = jnp.zeros_like(total_ref)

    batch, size = fringe_ref.shape[0], fringe_ref.shape[1]
    for i in range(batch):
        coef = coef_ref[0, :, i].astype(jnp.float32)
        coef = coef.reshape(-1, coef.shape[2]).astype(jnp.bfloat16)
        fitted = dot32(coef, basis_t_ref[...]) * weight_ref[i]
        group = ids_ref[item * batch + i]
        total_ref[group, :size] += fringe_ref[i].astype(jnp.float32) - fitted
        total_ref[group, size:] += jnp.ones_like(total_ref[group, size:])

    @pl.when(item == pl.num_programs(0) - 1)
    def _():
        out_ref[...] = total_ref[...].astype(jnp.bfloat16)


def newton_scales(low, high):
    scales = []
    value = (high + low) / (high - low)
    while True:
        doubled = 2.0 * value * value
        scales.append(doubled / (doubled - 1.0))
        value = doubled - 1.0
        if value > 1e6:
            return scales


def full(shape):
    return pl.BlockSpec(shape, lambda i, *rest: (0,) * len(shape))


def lead(shape):
    return pl.BlockSpec(shape, lambda i, *rest: (i,) + (0,) * (len(shape) - 1))


def second(shape):
    return pl.BlockSpec(shape, lambda i, *rest: (0, i) + (0,) * (len(shape) - 2))


def per_device_general(vis, flags, band, group_id):
    items, chan, _, length = vis.shape
    both = 2 * length
    shards = lax.axis_size("freq")
    owners = lax.axis_size("bl")
    groups = GPO * owners
    time_local = length // shards
    rows = 2 * time_local
    pair = 2 if items % 2 == 0 else 1
    chunks = 2 if rows % 32 == 0 else 1
    rows //= chunks
    size = both // chunks
    bf16, f32 = jnp.bfloat16, jnp.float32

    table = fourier_tables(length)
    forward = jnp.asarray(table)
    inverse_t = forward
    if chunks == 1:
        inverse_t = table.reshape(2, shards, time_local, both)
        inverse_t = jnp.asarray(np.transpose(inverse_t, (1, 0, 2, 3)).reshape(both, both))
    response = band_response(band, length, NBAND).reshape(items, 1, both)
    basis = make_basis(CH, DELAYS)
    basis_t = jnp.asarray(basis.T.copy())
    basis = jnp.asarray(basis)
    basis_local = lax.dynamic_slice_in_dim(basis, lax.axis_index("freq") * chan, chan, 0)
    weight = 1.0 - flags.astype(f32)
    weight_rows = weight.reshape(items, 1, chan)
    weight_half = weight.astype(bf16)
    if shards <= 8:
        pieces = [weight_half] + [
            lax.ppermute(weight_half, "freq", [(d, (d - j) % shards) for d in range(shards)])
            for j in range(1, shards)
        ]
        doubled = jnp.concatenate(pieces + pieces, axis=1)
        offset = (shards - lax.axis_index("freq")) % shards * chan
        weight_full = lax.dynamic_slice_in_dim(doubled, offset, CH, 1)
    else:
        weight_full = lax.all_gather(weight_half, "freq", axis=1, tiled=True)
        response, weight_full = lax.optimization_barrier((response, weight_full))
    weight_full = weight_full.reshape(items, 1, CH)

    fringe, projected = pl.pallas_call(
        functools.partial(filter_kernel, shards, chunks),
        grid=(items // pair,),
        in_specs=[
            lead((pair, chan, 2, length)), full((both, both)), full((both, both)),
            lead((pair, 1, both)), lead((pair, 1, chan)), full((chan, DELAYS)),
        ],
        out_specs=[lead((pair, both, chan)), second((shards, pair, chunks, rows, DELAYS))],
        out_shape=[
            jax.ShapeDtypeStruct((items, both, chan), bf16),
            jax.ShapeDtypeStruct((shards, items, chunks, rows, DELAYS), bf16),
        ],
        compiler_params=pltpu.CompilerParams(vmem_limit_bytes=BIG),
        cost_estimate=pl.CostEstimate(
            flops=4 * items * chan * both * both, bytes_accessed=4 * items * chan * both,
            transcendentals=0,
        ),
    )(vis, forward, inverse_t, response, weight_rows, basis_local)

    projected, weight_full = lax.optimization_barrier((projected, weight_full))
    ridge = CH / 64.0
    high = ridge + 1.05 * CH
    batch = 4 if items % 4 == 0 else 1
    inverse = pl.pallas_call(
        functools.partial(
            inverse_kernel, batch, ridge, newton_scales(ridge, high), 2.0 / (ridge + high)
        ),
        grid=(items // batch,),
        in_specs=[lead((batch, 1, CH)), full((CH, DELAYS)), full((DELAYS, CH))],
        out_specs=lead((batch, DELAYS, DELAYS)),
        out_shape=jax.ShapeDtypeStruct((items, DELAYS, DELAYS), f32),
        compiler_params=pltpu.CompilerParams(vmem_limit_bytes=BIG),
        cost_estimate=pl.CostEstimate(
            flops=20_000_000_000, bytes_accessed=4 * items * DELAYS * DELAYS, transcendentals=0
        ),
    )(weight_full, basis, basis_t)

    received = lax.all_to_all(projected, "freq", split_axis=0, concat_axis=0, tiled=True)
    coefficients = pl.pallas_call(
        functools.partial(solve_kernel, batch),
        grid=(items // batch,),
        in_specs=[
            second((shards, batch, chunks, rows, DELAYS)), lead((batch, DELAYS, DELAYS)),
        ],
        out_specs=[second((1, batch, rows, DELAYS))] * chunks,
        out_shape=[jax.ShapeDtypeStruct((1, items, rows, DELAYS), bf16)] * chunks,
        compiler_params=pltpu.CompilerParams(vmem_limit_bytes=BIG),
    )(received, inverse)
    basis_local_t = basis_local.T
    tall = size + 16

    def clean(h, gathered):
        return pl.pallas_call(
            clean_kernel,
            grid_spec=pltpu.PrefetchScalarGridSpec(
                num_scalar_prefetch=1,
                grid=(items // batch,),
                in_specs=[
                    pl.BlockSpec((batch, size, chan), lambda i, ids: (i, h, 0)),
                    pl.BlockSpec((1, shards, batch, rows, DELAYS), lambda i, ids: (0, 0, i, 0, 0)),
                    full((DELAYS, chan)),
                    lead((batch, 1, chan)),
                ],
                out_specs=full((groups, tall, chan)),
                scratch_shapes=[pltpu.VMEM((groups, tall, chan), f32)],
            ),
            out_shape=jax.ShapeDtypeStruct((groups, tall, chan), bf16),
            compiler_params=pltpu.CompilerParams(vmem_limit_bytes=58 * 1024 * 1024),
            cost_estimate=pl.CostEstimate(
                flops=2_000_000_000, bytes_accessed=4 * items * size * chan, transcendentals=0
            ),
        )(group_id, fringe, gathered, basis_local_t, weight_rows)

    pieces = []
    for h in range(chunks):
        part = coefficients[h]
        if h:
            part, sums = lax.optimization_barrier((part, sums))
        sums = clean(h, gather_chain(part, shards, 1, h))
        if h:
            sums, pieces[-1] = lax.optimization_barrier((sums, pieces[-1]))
        arrived = lax.all_to_all(sums, "bl", split_axis=0, concat_axis=0, tiled=True)
        total = jnp.sum(arrived.reshape(owners, GPO, tall, chan).astype(f32), 0)
        counts = jnp.maximum(total[:, size:size + 1, :1], 1.0)
        mean = (total[:, :size] / counts).astype(bf16).reshape(GPO, shards, rows, chan)
        pieces.append(jnp.transpose(mean, (1, 0, 2, 3)))
    if shards > 8:
        swapped = [
            lax.all_to_all(piece, "freq", split_axis=0, concat_axis=0, tiled=True)
            for piece in pieces
        ]
        swapped = [jnp.concatenate(list(piece), axis=-1) for piece in swapped]
    else:
        me = lax.axis_index("freq")
        swapped = []
        for piece in pieces:
            parts = [lax.dynamic_index_in_dim(piece, me, 0, keepdims=False)]
            for j in range(1, shards):
                out = lax.dynamic_index_in_dim(piece, (me + shards - j) % shards, 0, keepdims=False)
                parts.append(
                    lax.ppermute(out, "freq", [(d, (d - j) % shards) for d in range(shards)])
                )
            doubled = jnp.concatenate(parts + parts, axis=-1)
            offset = (shards - me) % shards * chan
            swapped.append(lax.dynamic_slice_in_dim(doubled, offset, CH, 2))
    averaged = [piece.reshape(GPO, 2 // chunks, time_local, CH) for piece in swapped]
    return jnp.concatenate(averaged, 1)


MESH = pl.DeviceIdType.MESH
RANK = 48


def filter_tables(length, shards):
    sample_index = np.arange(length)
    phase_index = sample_index[:, None] * sample_index[None, :] % length
    angles = phase_index.astype(np.float32) * np.float32(2.0 * math.pi / length)
    cosine = np.cos(angles).astype(jnp.bfloat16).astype(np.float64)
    sine = np.sin(angles).astype(jnp.bfloat16).astype(np.float64)
    signed = (sample_index - length * (sample_index >= length // 2)).astype(np.float64)
    tables = []
    for band in range(NBAND):
        center = (band - (NBAND - 1) / 2.0) * (length / (4.0 * NBAND))
        ratio = (signed - center) / (length / 32.0)
        response = (0.15 + 0.85 / (1.0 + ratio**4)) / length
        even = (cosine * response) @ cosine + (sine * response) @ sine
        odd = (cosine * response) @ sine - (sine * response) @ cosine
        whole = np.concatenate(
            [np.concatenate([even, odd], 1), np.concatenate([-odd, even], 1)], 0
        )
        tables.append(whole)
    tables = np.stack(tables).reshape(NBAND, 2 * length, 2, shards, length // shards)
    tables = np.transpose(tables, (3, 0, 1, 2, 4))
    return tables.reshape(shards, NBAND, 2 * length, 2 * length // shards).astype(jnp.bfloat16)


def factored_basis(channels, modes, shards):
    size = channels // shards
    channel_index = np.arange(channels)
    order_index = np.arange(modes)
    phase = (order_index[None, :] * (2 * channel_index[:, None] + 1) % (4 * channels)).astype(
        np.longdouble
    )
    exact = np.cos(phase * (np.longdouble(np.pi) / (2 * channels)))
    fronts, backs = [], []
    for z in range(shards):
        block = exact[z * size:(z + 1) * size]
        rest = block.copy()
        columns = []
        for _ in range(RANK):
            norms = (rest * rest).sum(0)
            best = int(np.argmax(norms))
            column = rest[:, best] / np.sqrt(norms[best])
            for other in columns:
                column = column - other * (other * column).sum()
            column = column / np.sqrt((column * column).sum())
            columns.append(column)
            rest = rest - column[:, None] * (column[:, None] * rest).sum(0)[None]
        front = np.stack(columns)
        fronts.append(front)
        backs.append(np.stack([(row[:, None] * block).sum(0) for row in front]))
    fronts = np.stack(fronts).astype(np.float32)
    spread = np.zeros((shards, 2, RANK, size, 2), np.float32)
    for r in range(2):
        spread[:, r, :, :, r] = fronts
    fronts = spread.reshape(shards, 2 * RANK, 2 * size).astype(jnp.bfloat16)
    backs = np.concatenate(backs).astype(np.float32).astype(jnp.bfloat16)
    return fronts, backs.T.copy()


def dot_nt(left, right):
    return lax.dot_general(left, right, NT, preferred_element_type=jnp.float32)


def main_kernel(ridge, scales, start_scale, ids, bands, vis_hbm, flags_ref, m_hbm, front_hbm,
                back_ref, basis_hbm, basis_t_hbm, out_ref,
                vis_v, m_v, front_v, basis_v, basis_t_v, sep_a, sep_b, pick_a, pick_b, weight_v, half_v, spread_v, turned_v, sums_a, sums_b,
                pair_send_a, pair_send_b, pair_recv_a, pair_recv_b, cross_send_a, cross_send_b,
                cross_recv_a, cross_recv_b, far_send_a, far_send_b, far_recv_a, far_recv_b,
                y_send, y_recv, w_recv, wide, inv_v, coef_v, coef_send, coef_recv,
                code_tmp, code_send, code_recv, left_v, right_v, fit_v,
                prev_s, last_s, next_s, slot_s, local_sem, send_sem, recv_sem):
    f32, bf16 = jnp.float32, jnp.bfloat16
    items, chan = vis_v.shape[0], vis_v.shape[1]
    length = vis_v.shape[3]
    rt = m_v.shape[3]
    modes = basis_v.shape[1]
    me_b, me_f = lax.axis_index("bl"), lax.axis_index("freq")
    me_x, me_c = me_b // 2, lax.rem(me_b, 2)
    far = [lax.rem(me_f + 2, 4), 3 - me_f, me_f + 1 - 2 * lax.rem(me_f, 2), me_f]
    sibling = me_b + 1 - 2 * me_c
    across = lax.rem(me_b + 2, 4)
    diagonal = 3 - me_b
    owners = [me_b, sibling, across, diagonal]
    sums = (sums_a, sums_b)
    pair_send, pair_recv = (pair_send_a, pair_send_b), (pair_recv_a, pair_recv_b)
    cross_send, cross_recv = (cross_send_a, cross_send_b), (cross_recv_a, cross_recv_b)
    far_send, far_recv = (far_send_a, far_send_b), (far_recv_a, far_recv_b)
    spans = [(0, sums_a.shape[1]), (sums_a.shape[1], sums_b.shape[1])]
    chunk = items // 4

    def load(i):
        return pltpu.make_async_copy(
            vis_hbm.at[pl.ds(i * chunk, chunk)], vis_v.at[pl.ds(i * chunk, chunk)],
            local_sem.at[i],
        )

    tables = [
        pltpu.make_async_copy(m_hbm.at[far[j]], m_v.at[j], local_sem.at[4 + j])
        for j in range(4)
    ]
    bases = [
        pltpu.make_async_copy(basis_hbm, basis_v, local_sem.at[8]),
        pltpu.make_async_copy(basis_t_hbm, basis_t_v, local_sem.at[9]),
    ]
    front = pltpu.make_async_copy(front_hbm.at[me_f], front_v, local_sem.at[10])
    for copy in [load(0), front] + tables + [load(i) for i in range(1, 4)]:
        copy.start()

    barrier = pltpu.get_barrier_semaphore()
    for j in range(3):
        pl.semaphore_signal(barrier, inc=1, device_id={"freq": far[j]}, device_id_type=MESH)
        pl.semaphore_signal(barrier, inc=1, device_id={"bl": owners[j + 1]}, device_id_type=MESH)

    weight_v[...] = 1.0 - flags_ref[...].astype(f32)
    half_v[...] = weight_v[...].astype(bf16)
    repeat = (
        lax.broadcasted_iota(jnp.int32, (chan, 2 * chan), 1) // 2
        == lax.broadcasted_iota(jnp.int32, (chan, 2 * chan), 0)
    ).astype(f32)
    spread_v[...] = dot32(half_v[...], repeat.astype(bf16))
    padded = jnp.concatenate([weight_v[...], jnp.zeros((128 - items, chan), f32)], 0)
    turned_v[...] = padded.T.astype(bf16)
    for total in sums:
        total[0] = jnp.zeros_like(total[0])
    group = [ids[b] for b in range(items)]
    for b in range(items):
        before, after = jnp.int32(0), jnp.int32(items)
        for other in range(b):
            before = jnp.where(group[other] == group[b], other + 1, before)
        for other in reversed(range(b + 1, items)):
            after = jnp.where(group[other] // GPO == group[b] // GPO, other, after)
        prev_s[b] = before
        next_s[b] = after
    next_s[items] = jnp.int32(items)
    for g in range(4 * GPO):
        end = jnp.int32(0)
        for b in range(items):
            end = jnp.where(group[b] == g, b + 1, end)
        last_s[g] = end
    for o in range(4):
        place = jnp.int32(items)
        for b in reversed(range(items)):
            place = jnp.where(group[b] // GPO == o, b, place)
        for step in range(CAP):
            slot_s[o * CAP + step] = place
            place = next_s[place]

    pl.semaphore_wait(barrier, 6)

    pending = []

    def remote(index, source, target, axis, place):
        return pltpu.make_async_remote_copy(
            src_ref=source, dst_ref=target, send_sem=send_sem.at[index],
            recv_sem=recv_sem.at[index], device_id={axis: place}, device_id_type=MESH,
        )

    def send(index, source, target, axis, place):
        copy = remote(index, source, target, axis, place)
        copy.start()
        pending.append(copy)
        return copy

    def y_copy(j, c):
        part = pl.ds(c * chunk, chunk)
        return remote(
            31 + 4 * j + c, y_send.at[j, part], y_recv.at[me_f, part], "freq", far[j]
        )

    w_copies = [send(j, half_v, w_recv.at[me_f], "freq", far[j]) for j in range(3)]

    def separate(b, span, target, pick):
        at, size = span
        values = vis_v[b, at:at + size].astype(f32).reshape(2 * size, length)
        for h in range(length // 128):
            pick[h, :2 * size] = values[:, h * 128:(h + 1) * 128]
        chosen = (lax.broadcasted_iota(jnp.int32, (128, 128), 0) == b).astype(f32).astype(bf16)
        mask = dot32(turned_v[at:at + size], chosen)
        for r in range(2):
            for h in range(length // 128):
                place = r * length + h * 128
                target[:size, place:place + 128] = (
                    pick[h, pl.ds(r, size, stride=2), :] * mask
                ).astype(bf16)

    def table_of(b):
        return jnp.concatenate([m_v[j, bands[b]] for j in range(4)], 1)

    def project(b, target, at):
        rows = vis_v[b].reshape(2 * chan, length)
        picked = front_v[...] * spread_v[pl.ds(b, 1), :].astype(bf16)
        raw = dot32(picked, rows).astype(bf16)
        target[at:at + RANK, :length] = raw[:RANK]
        target[at:at + RANK, length:] = raw[RANK:]

    def filter_one(b, q, source):
        size = spans[q][1]
        rows = size + RANK if q == 0 else size
        fringe = dot32(source[:rows], table_of(b))
        sums[q][b + 1] = sums[q][prev_s[b]] + fringe[:size]
        if q == 0:
            y = fringe[size:].astype(bf16)
            for j in range(3):
                y_send[j, b] = y[:, j * rt:(j + 1) * rt]
            y_recv[me_f, b] = y[:, 3 * rt:]

    for table in tables:
        table.wait()
    front.wait()

    def project_chunk(c, carry):
        load(c).wait()
        for i in range(chunk):
            target, pick = ((sep_a, pick_a), (sep_b, pick_b))[i % 2]
            separate(c * chunk + i, spans[0], target, pick)
            project(c * chunk + i, target, spans[0][1])
            filter_one(c * chunk + i, 0, target)
        for j in range(3):
            y_copy(j, c).start()
        return carry

    lax.fori_loop(0, 4, project_chunk, 0)
    for copy in bases:
        copy.start()

    pair_copies, cross_copies, far_copies = [[], []], [[], []], []

    def filter_span(q, first, last):
        def filter_pair(t, carry):
            separate(2 * t + 1, spans[q], sep_b, pick_b)
            filter_one(2 * t, q, sep_a)
            separate(jnp.minimum(2 * t + 2, items - 1), spans[q], sep_a, pick_a)
            filter_one(2 * t + 1, q, sep_b)
            return carry

        lax.fori_loop(first, last, filter_pair, 0)

    def pair_start(q):
        for j in range(4):
            for x in range(2):
                for l in range(GPO):
                    g = GPO * (2 * x + 1 - me_c) + l
                    part = sums[q][last_s[g], :, j * rt:(j + 1) * rt]
                    pair_send[q][j, GPO * x + l] = part.astype(bf16)
            pair_copies[q].append(
                send(3 + 4 * q + j, pair_send[q].at[j], pair_recv[q].at[j], "bl", sibling)
            )

    def pair_stage(q):
        for j in range(4):
            pair_copies[q][j].wait_recv()
            for l in range(GPO):
                mine = sums[q][last_s[GPO * across + l], :, j * rt:(j + 1) * rt]
                other = pair_recv[q][j, GPO * (1 - me_x) + l].astype(f32)
                cross_send[q][j, l] = (mine + other).astype(bf16)
            cross_copies[q].append(
                send(11 + 4 * q + j, cross_send[q].at[j], cross_recv[q].at[j], "bl", across)
            )

    def cross_stage(q, j):
        cross_copies[q][j].wait_recv()
        for l in range(GPO):
            total = sums[q][last_s[GPO * me_b + l], :, j * rt:(j + 1) * rt]
            total = total + pair_recv[q][j, GPO * me_x + l].astype(f32)
            total = (total + cross_recv[q][j, l].astype(f32)).astype(bf16)
            if j < 3:
                far_send[q][j, l] = total
            else:
                far_recv[q][me_f, l] = total
        if j < 3:
            far_copies.append(
                send(19 + 3 * q + j, far_send[q].at[j], far_recv[q].at[me_f], "freq", far[j])
            )

    pair_start(0)
    separate(0, spans[1], sep_a, pick_a)
    filter_span(1, 0, 2)
    pair_stage(0)
    filter_span(1, 2, items // 2)
    pair_start(1)

    for copy in w_copies:
        copy.wait_recv()
    w_recv[me_f] = half_v[...]
    for z in range(4):
        wide[:items, z * chan:(z + 1) * chan] = w_recv[z].astype(f32)
    wide[items:, :] = jnp.zeros_like(wide[items:, :])

    half = wide.shape[1] // 2
    code_copies = []
    for k in range(4):
        for s in range(CAP):
            place = slot_s[owners[k] * CAP + s]
            local = lax.rem(ids[jnp.minimum(place, items - 1)], GPO) + 1
            code = jnp.where(place < items, local, 0).astype(f32)
            row = wide[pl.ds(place, 1), :] * code
            for h in range(2):
                code_tmp[h * CAP + s:h * CAP + s + 1, :half] = row[:, h * half:(h + 1) * half]
                code_tmp[h * CAP + s:h * CAP + s + 1, half:] = (
                    jnp.zeros((1, code_tmp.shape[1] - half), f32) + code
                )
        if k == 0:
            code_recv[me_b] = code_tmp[...].astype(bf16)
        else:
            code_send[k - 1] = code_tmp[...].astype(bf16)
            code_copies.append(
                send(24 + k, code_send.at[k - 1], code_recv.at[me_b], "bl", owners[k])
            )

    for copy in bases:
        copy.wait()
    eye = (
        lax.broadcasted_iota(jnp.int32, (modes, modes), 0)
        == lax.broadcasted_iota(jnp.int32, (modes, modes), 1)
    ).astype(f32)
    batch = 8

    def invert(step, carry):
        normals = []
        for i in range(batch):
            weight = wide[pl.ds(step * batch + i, 1), :].astype(bf16)
            normals.append(dot32(basis_t_v[...] * weight, basis_v[...]) + ridge * eye)
        guess = [
            scales[0] * (2.0 * start_scale * eye - start_scale * start_scale * normal)
            for normal in normals
        ]
        normals = [halves(normal) for normal in normals]
        for turn, scale in enumerate(scales[1:]):
            parts = [halves(value) for value in guess]
            if turn + 3 < len(scales) - 1:
                product = [dot32(n[0], g[0]) for n, g in zip(normals, parts)]
            else:
                product = [dot_split(n, g) for n, g in zip(normals, parts)]
            error = [(eye - value).astype(bf16) for value in product]
            guess = [
                scale * (value + dot32(g[0], e)) for value, g, e in zip(guess, parts, error)
            ]
        for i in range(batch):
            inv_v[step * batch + i] = guess[i]
        return carry

    for j in range(4):
        cross_stage(0, j)
    pair_stage(1)
    for j in range(items // batch):
        lax.fori_loop(j, j + 1, invert, 0)
        if j == 0:
            cross_stage(1, 0)
            cross_stage(1, 1)
    cross_stage(1, 2)

    def solve(p, carry):
        values = y_recv[:, p].reshape(-1, rt)
        projected = dot32(back_ref[...], values).T
        coef_v[p] = dot_split(halves(projected), halves(inv_v[p])).astype(bf16)
        return carry

    for c in range(4):
        for j in range(3):
            y_copy(j, c).wait_recv()
        lax.fori_loop(c * chunk, (c + 1) * chunk, solve, 0, unroll=4)
    coef_v[items] = jnp.zeros_like(coef_v[items])
    coef_copies = []
    for k in (2, 3, 1, 0):
        for s in range(CAP):
            value = coef_v[slot_s[owners[k] * CAP + s]]
            if k == 0:
                coef_recv[me_b, s] = value
            else:
                coef_send[k - 1, s] = value
        if k > 0:
            coef_copies.append(
                send(27 + k, coef_send.at[k - 1], coef_recv.at[me_b], "bl", owners[k])
            )

    counts = [jnp.zeros((1, 128), f32) for _ in range(GPO)]
    for k in range(4):
        if k == 3:
            cross_stage(1, 3)
            for copy in far_copies:
                copy.wait_recv()
            for l in range(GPO):
                for z in range(4):
                    for q, (low, size) in enumerate(spans):
                        at = z * chan + low
                        rest = far_recv[q][z, l].astype(f32).T
                        fit_v[l * rt:(l + 1) * rt, at:at + size] = (
                            rest - fit_v[l * rt:(l + 1) * rt, at:at + size]
                        )
        if k > 0:
            code_copies[k - 1].wait_recv()
            coef_copies[{1: 2, 2: 0, 3: 1}[k]].wait_recv()
        place = owners[k]
        codes = code_recv[place].astype(f32)
        for s in range(CAP):
            value = coef_recv[place, s].astype(f32)
            for l in range(GPO):
                match = (codes[s:s + 1, half:half + 128] == 1.0 + l).astype(f32)
                counts[l] = counts[l] + match
                left_v[l * rt:(l + 1) * rt, s * modes:(s + 1) * modes] = (value * match).astype(
                    bf16
                )
        for h in range(2):
            for s in range(CAP):
                row = codes[h * CAP + s:h * CAP + s + 1, :half]
                weight = (row > 0.0).astype(f32).astype(bf16)
                right_v[s * modes:(s + 1) * modes, :] = (
                    basis_t_v[:, h * half:(h + 1) * half] * weight
                )
            fitted = dot32(left_v[...], right_v[...])
            if k == 0:
                fit_v[:, h * half:(h + 1) * half] = fitted
            elif k == 3:
                for l in range(GPO):
                    share = 1.0 / jnp.maximum(counts[l][:, :1], 1.0)
                    rest = fit_v[l * rt:(l + 1) * rt, h * half:(h + 1) * half]
                    rest = rest - fitted[l * rt:(l + 1) * rt]
                    out_ref[l, :, h * half:(h + 1) * half] = (rest * share).astype(bf16)
            else:
                fit_v[:, h * half:(h + 1) * half] = fit_v[:, h * half:(h + 1) * half] + fitted

    for c in range(4):
        for j in range(3):
            y_copy(j, c).wait_send()
    for copy in pending:
        copy.wait_send()


def per_device_fused(vis, flags, band, group_id):
    items, chan, _, length = vis.shape
    shards = 4
    f32, bf16 = jnp.float32, jnp.bfloat16
    rt = 2 * length // shards
    channels = chan * shards
    smem = pl.BlockSpec(memory_space=pltpu.SMEM)
    vmem = pl.BlockSpec(memory_space=pltpu.VMEM)
    hbm = pl.BlockSpec(memory_space=pltpu.HBM)
    table = jnp.asarray(filter_tables(length, shards))
    fronts, backs = factored_basis(channels, DELAYS, shards)
    basis = make_basis(channels, DELAYS)
    ridge = channels / 64.0
    high = ridge + 1.05 * channels
    half = channels // 2
    narrow = 128
    out = pl.pallas_call(
        functools.partial(main_kernel, ridge, newton_scales(ridge, high), 2.0 / (ridge + high)),
        in_specs=[smem, smem, hbm, vmem, hbm, hbm, vmem, hbm, hbm],
        out_specs=vmem,
        out_shape=jax.ShapeDtypeStruct((GPO, rt, channels), bf16),
        scratch_shapes=[
            pltpu.VMEM(vis.shape, bf16),
            pltpu.VMEM((shards, NBAND, 2 * length, rt), bf16),
            pltpu.VMEM((2 * RANK, 2 * chan), bf16),
            pltpu.VMEM((channels, DELAYS), bf16),
            pltpu.VMEM((DELAYS, channels), bf16),
            pltpu.VMEM((chan, 2 * length), bf16),
            pltpu.VMEM((chan, 2 * length), bf16),
            pltpu.VMEM((length // 128, 2 * chan, 128), f32),
            pltpu.VMEM((length // 128, 2 * chan, 128), f32),
            pltpu.VMEM((items, chan), f32),
            pltpu.VMEM((items, chan), bf16),
            pltpu.VMEM((items, 2 * chan), f32),
            pltpu.VMEM((chan, 128), bf16),
            pltpu.VMEM((items + 1, narrow, 2 * length), f32),
            pltpu.VMEM((items + 1, chan - narrow, 2 * length), f32),
        ] + [
            pltpu.VMEM(lead_shape + (size, rt), bf16)
            for lead_shape in ((4, 2 * GPO), (4, 2 * GPO), (4, GPO), (4, GPO), (3, GPO), (shards, GPO))
            for size in (narrow, chan - narrow)
        ] + [
            pltpu.VMEM((3, items, RANK, rt), bf16),
            pltpu.VMEM((shards, items, RANK, rt), bf16),
            pltpu.VMEM((shards, items, chan), bf16),
            pltpu.VMEM((items + 8, channels), f32),
            pltpu.VMEM((items, DELAYS, DELAYS), f32),
            pltpu.VMEM((items + 1, rt, DELAYS), bf16),
            pltpu.VMEM((3, CAP, rt, DELAYS), bf16),
            pltpu.VMEM((4, CAP, rt, DELAYS), bf16),
            pltpu.VMEM((2 * CAP, half + 128), f32),
            pltpu.VMEM((3, 2 * CAP, half + 128), bf16),
            pltpu.VMEM((4, 2 * CAP, half + 128), bf16),
            pltpu.VMEM((GPO * rt, CAP * DELAYS), bf16),
            pltpu.VMEM((CAP * DELAYS, half), bf16),
            pltpu.VMEM((GPO * rt, channels), f32),
            pltpu.SMEM((items,), jnp.int32),
            pltpu.SMEM((4 * GPO,), jnp.int32),
            pltpu.SMEM((items + 1,), jnp.int32),
            pltpu.SMEM((4 * CAP,), jnp.int32),
            pltpu.SemaphoreType.DMA((11,)),
            pltpu.SemaphoreType.DMA((43,)),
            pltpu.SemaphoreType.DMA((43,)),
        ],
        compiler_params=pltpu.CompilerParams(
            collective_id=0, has_side_effects=True, vmem_limit_bytes=56 * 1024 * 1024
        ),
        cost_estimate=pl.CostEstimate(
            flops=10_000_000_000, bytes_accessed=4 * vis.size, transcendentals=0
        ),
    )(
        group_id, band, vis, flags, table, jnp.asarray(fronts), jnp.asarray(backs),
        jnp.asarray(basis), jnp.asarray(basis.T.copy()),
    )
    return out.reshape(GPO, 2, length // shards, channels)


def per_device(vis, flags, band, group_id):
    items, chan, _, length = vis.shape
    fits = (
        lax.axis_size("freq") == 4 and lax.axis_size("bl") == 4 and items == 16
        and chan % 128 == 0 and chan > 128 and length == 256
    )
    return (per_device_fused if fits else per_device_general)(vis, flags, band, group_id)


def solution(mesh):
    in_specs = (P("bl", "freq", None, "win"), P("bl", "freq"), P("bl"), P("bl"))
    out_specs = P("bl", None, ("win", "freq"), None)
    return jax.shard_map(
        per_device, mesh=mesh, in_specs=in_specs, out_specs=out_specs, check_vma=False
    )
```

```python
import functools
import math

import jax
import jax.numpy as jnp
import numpy as np
from jax import lax
from jax.experimental import pallas as pl
from jax.experimental.pallas import tpu as pltpu
from jax.sharding import PartitionSpec as P

CH = 1536
DELAYS = 128
NBAND = 8
GPO = 2
CAP = 8


def fourier_tables(length):
    sample_index = np.arange(length, dtype=np.int32)
    phase_index = sample_index[:, None] * sample_index[None, :] % length
    angles = phase_index.astype(np.float32) * np.float32(2.0 * math.pi / length)
    cosine = np.cos(angles)
    sine_table = np.sin(angles)
    forward = np.concatenate(
        [np.concatenate([cosine, -sine_table], 1), np.concatenate([sine_table, cosine], 1)], 0
    )
    return forward.astype(jnp.bfloat16)


def band_response(band, length, band_count):
    mode_index = jnp.arange(length, dtype=jnp.int32)
    signed_modes = (mode_index - length * (mode_index >= length // 2).astype(jnp.int32)).astype(
        jnp.float32
    )
    center = (band.astype(jnp.float32) - (band_count - 1) / 2.0) * (length / (4.0 * band_count))
    band_width = length / 32.0
    offset_ratio = (signed_modes[None, :] - center[:, None]) / band_width
    single = (0.15 + 0.85 / (1.0 + offset_ratio**4)) / length
    return jnp.concatenate([single, single], 1)


def make_basis(channels, modes):
    channel_index = np.arange(channels, dtype=np.int32)
    order_index = np.arange(modes, dtype=np.int32)
    phase_index = order_index[None, :] * (2 * channel_index[:, None] + 1) % (4 * channels)
    return np.cos(phase_index.astype(np.float32) * np.float32(math.pi / (2 * channels))).astype(
        jnp.bfloat16
    )


NT = (((1,), (1,)), ((), ()))
BIG = 48 * 1024 * 1024


def dot32(left, right):
    return jnp.dot(left, right, preferred_element_type=jnp.float32)


def halves(value):
    high = value.astype(jnp.bfloat16)
    return high, (value - high.astype(jnp.float32)).astype(jnp.bfloat16)


def dot_split(left, right):
    left_high, left_low = left
    right_high, right_low = right
    return dot32(left_high, right_high) + (
        dot32(left_high, right_low) + dot32(left_low, right_high)
    )


def filter_kernel(shards, chunks, vis_ref, fwd_ref, inv_ref, resp_ref, weight_ref, basis_ref,
                  fringe_ref, proj_ref):
    batch, half = vis_ref.shape[0], vis_ref.shape[3]
    spectra = [
        dot32(vis_ref[i, :, 0, :], fwd_ref[:half]) + dot32(vis_ref[i, :, 1, :], fwd_ref[half:])
        for i in range(batch)
    ]
    spectra = [(spectra[i] * resp_ref[i]).astype(jnp.bfloat16) for i in range(batch)]
    for i in range(batch):
        fringe = lax.dot_general(inv_ref[...], spectra[i], NT, preferred_element_type=jnp.float32)
        fringe = (fringe * weight_ref[i]).astype(jnp.bfloat16)
        fringe_ref[i] = fringe
        projected = dot32(fringe, basis_ref[...])
        size = projected.shape[0] // chunks
        for h in range(chunks):
            piece = projected[h * size:(h + 1) * size].reshape(shards, -1, projected.shape[1])
            proj_ref[:, i, h] = piece.astype(jnp.bfloat16)


def inverse_kernel(batch, ridge, scales, start, weight_ref, basis_ref, basis_t_ref, out_ref):
    modes = out_ref.shape[1]
    eye = (
        lax.broadcasted_iota(jnp.int32, (modes, modes), 0)
        == lax.broadcasted_iota(jnp.int32, (modes, modes), 1)
    ).astype(jnp.float32)
    normals = [
        dot32(basis_t_ref[...] * weight_ref[i], basis_ref[...]) + ridge * eye for i in range(batch)
    ]
    first = scales[0]
    guess = [first * (2.0 * start * eye - start * start * normal) for normal in normals]
    normals = [halves(normal) for normal in normals]
    for scale in scales[1:]:
        guess_parts = [halves(value) for value in guess]
        product = [dot_split(n, g) for n, g in zip(normals, guess_parts)]
        change = [halves(2.0 * eye - value) for value in product]
        guess = [scale * dot_split(g, c) for g, c in zip(guess_parts, change)]
    for i in range(batch):
        out_ref[i] = guess[i]


def solve_kernel(batch, recv_ref, inverse_ref, *out_refs):
    for i in range(batch):
        inverse = halves(inverse_ref[i])
        for h, out_ref in enumerate(out_refs):
            total = jnp.sum(recv_ref[:, i, h].astype(jnp.float32), axis=0)
            out_ref[0, i] = dot_split(halves(total), inverse).astype(jnp.bfloat16)


def chain_kernel(shards, chunks, own_ref, out_ref, send_sem, recv_sem):
    me = lax.axis_index("freq")
    has_right, has_left = me < shards - 1, me > 0
    barrier = pltpu.get_barrier_semaphore()

    def greet(has, step):
        @pl.when(has)
        def _():
            pl.semaphore_signal(
                barrier, inc=1, device_id={"freq": me + step},
                device_id_type=pl.DeviceIdType.MESH,
            )

    greet(has_right, 1)
    greet(has_left, -1)
    pl.semaphore_wait(barrier, has_right.astype(jnp.int32) + has_left.astype(jnp.int32))

    def copy(way, h, hop, step):
        source = me - step * hop
        start = own_ref.at[h] if hop == 0 else out_ref.at[h, source]
        return pltpu.make_async_remote_copy(
            src_ref=start,
            dst_ref=out_ref.at[h, source],
            send_sem=send_sem.at[way, h, hop],
            recv_sem=recv_sem.at[way, h, hop],
            device_id={"freq": me + step},
            device_id_type=pl.DeviceIdType.MESH,
        )

    def arrival(way, h, hop, step):
        source = me - step * (hop + 1)
        return pltpu.make_async_remote_copy(
            src_ref=own_ref.at[h],
            dst_ref=out_ref.at[h, source],
            send_sem=send_sem.at[way, h, hop],
            recv_sem=recv_sem.at[way, h, hop],
            device_id={"freq": me - step},
            device_id_type=pl.DeviceIdType.MESH,
        )

    ways = ((0, 1, has_right), (1, -1, has_left))
    for hop in range(shards):
        for h in range(chunks):
            for way, step, has in ways:
                source = me - step * hop
                held = jnp.logical_and(source >= 0, source <= shards - 1)
                if hop > 0:
                    @pl.when(held)
                    def _():
                        arrival(way, h, hop - 1, step).wait_recv()
                if hop < shards - 1:
                    @pl.when(jnp.logical_and(held, has))
                    def _():
                        copy(way, h, hop, step).start()
        if hop == 0:
            for h in range(chunks):
                out_ref[h, me] = own_ref[h]
    for hop in range(shards - 1):
        for h in range(chunks):
            for way, step, has in ways:
                source = me - step * hop
                held = jnp.logical_and(source >= 0, source <= shards - 1)

                @pl.when(jnp.logical_and(held, has))
                def _():
                    copy(way, h, hop, step).wait_send()


def gather_chain(part, shards, chunks, call):
    if shards > 8:
        return jnp.stack([lax.all_gather(part[h], "freq") for h in range(chunks)])
    hops = max(shards - 1, 1)
    return pl.pallas_call(
        functools.partial(chain_kernel, shards, chunks),
        in_specs=[pl.BlockSpec(memory_space=pltpu.VMEM)],
        out_specs=pl.BlockSpec(memory_space=pltpu.VMEM),
        out_shape=jax.ShapeDtypeStruct((chunks, shards) + part.shape[1:], part.dtype),
        scratch_shapes=[
            pltpu.SemaphoreType.DMA((2, chunks, hops)),
            pltpu.SemaphoreType.DMA((2, chunks, hops)),
        ],
        compiler_params=pltpu.CompilerParams(
            collective_id=call, has_side_effects=True, vmem_limit_bytes=58 * 1024 * 1024
        ),
        cost_estimate=pl.CostEstimate(
            flops=20_000_000_000, bytes_accessed=2 * shards * part.size, transcendentals=0
        ),
    )(part)


def clean_kernel(ids_ref, fringe_ref, coef_ref, basis_t_ref, weight_ref, out_ref, total_ref):
    item = pl.program_id(0)

    @pl.when(item == 0)
    def _():
        total_ref[...] = jnp.zeros_like(total_ref)

    batch, size = fringe_ref.shape[0], fringe_ref.shape[1]
    for i in range(batch):
        coef = coef_ref[0, :, i].astype(jnp.float32)
        coef = coef.reshape(-1, coef.shape[2]).astype(jnp.bfloat16)
        fitted = dot32(coef, basis_t_ref[...]) * weight_ref[i]
        group = ids_ref[item * batch + i]
        total_ref[group, :size] += fringe_ref[i].astype(jnp.float32) - fitted
        total_ref[group, size:] += jnp.ones_like(total_ref[group, size:])

    @pl.when(item == pl.num_programs(0) - 1)
    def _():
        out_ref[...] = total_ref[...].astype(jnp.bfloat16)


def newton_scales(low, high):
    scales = []
    value = (high + low) / (high - low)
    while True:
        doubled = 2.0 * value * value
        scales.append(doubled / (doubled - 1.0))
        value = doubled - 1.0
        if value > 1e6:
            return scales


def full(shape):
    return pl.BlockSpec(shape, lambda i, *rest: (0,) * len(shape))


def lead(shape):
    return pl.BlockSpec(shape, lambda i, *rest: (i,) + (0,) * (len(shape) - 1))


def second(shape):
    return pl.BlockSpec(shape, lambda i, *rest: (0, i) + (0,) * (len(shape) - 2))


def per_device_general(vis, flags, band, group_id):
    items, chan, _, length = vis.shape
    both = 2 * length
    shards = lax.axis_size("freq")
    owners = lax.axis_size("bl")
    groups = GPO * owners
    time_local = length // shards
    rows = 2 * time_local
    pair = 2 if items % 2 == 0 else 1
    chunks = 2 if rows % 32 == 0 else 1
    rows //= chunks
    size = both // chunks
    bf16, f32 = jnp.bfloat16, jnp.float32

    table = fourier_tables(length)
    forward = jnp.asarray(table)
    inverse_t = forward
    if chunks == 1:
        inverse_t = table.reshape(2, shards, time_local, both)
        inverse_t = jnp.asarray(np.transpose(inverse_t, (1, 0, 2, 3)).reshape(both, both))
    response = band_response(band, length, NBAND).reshape(items, 1, both)
    basis = make_basis(CH, DELAYS)
    basis_t = jnp.asarray(basis.T.copy())
    basis = jnp.asarray(basis)
    basis_local = lax.dynamic_slice_in_dim(basis, lax.axis_index("freq") * chan, chan, 0)
    weight = 1.0 - flags.astype(f32)
    weight_rows = weight.reshape(items, 1, chan)
    weight_half = weight.astype(bf16)
    if shards <= 8:
        pieces = [weight_half] + [
            lax.ppermute(weight_half, "freq", [(d, (d - j) % shards) for d in range(shards)])
            for j in range(1, shards)
        ]
        doubled = jnp.concatenate(pieces + pieces, axis=1)
        offset = (shards - lax.axis_index("freq")) % shards * chan
        weight_full = lax.dynamic_slice_in_dim(doubled, offset, CH, 1)
    else:
        weight_full = lax.all_gather(weight_half, "freq", axis=1, tiled=True)
        response, weight_full = lax.optimization_barrier((response, weight_full))
    weight_full = weight_full.reshape(items, 1, CH)

    fringe, projected = pl.pallas_call(
        functools.partial(filter_kernel, shards, chunks),
        grid=(items // pair,),
        in_specs=[
            lead((pair, chan, 2, length)), full((both, both)), full((both, both)),
            lead((pair, 1, both)), lead((pair, 1, chan)), full((chan, DELAYS)),
        ],
        out_specs=[lead((pair, both, chan)), second((shards, pair, chunks, rows, DELAYS))],
        out_shape=[
            jax.ShapeDtypeStruct((items, both, chan), bf16),
            jax.ShapeDtypeStruct((shards, items, chunks, rows, DELAYS), bf16),
        ],
        compiler_params=pltpu.CompilerParams(vmem_limit_bytes=BIG),
        cost_estimate=pl.CostEstimate(
            flops=4 * items * chan * both * both, bytes_accessed=4 * items * chan * both,
            transcendentals=0,
        ),
    )(vis, forward, inverse_t, response, weight_rows, basis_local)

    projected, weight_full = lax.optimization_barrier((projected, weight_full))
    ridge = CH / 64.0
    high = ridge + 1.05 * CH
    batch = 4 if items % 4 == 0 else 1
    inverse = pl.pallas_call(
        functools.partial(
            inverse_kernel, batch, ridge, newton_scales(ridge, high), 2.0 / (ridge + high)
        ),
        grid=(items // batch,),
        in_specs=[lead((batch, 1, CH)), full((CH, DELAYS)), full((DELAYS, CH))],
        out_specs=lead((batch, DELAYS, DELAYS)),
        out_shape=jax.ShapeDtypeStruct((items, DELAYS, DELAYS), f32),
        compiler_params=pltpu.CompilerParams(vmem_limit_bytes=BIG),
        cost_estimate=pl.CostEstimate(
            flops=20_000_000_000, bytes_accessed=4 * items * DELAYS * DELAYS, transcendentals=0
        ),
    )(weight_full, basis, basis_t)

    received = lax.all_to_all(projected, "freq", split_axis=0, concat_axis=0, tiled=True)
    coefficients = pl.pallas_call(
        functools.partial(solve_kernel, batch),
        grid=(items // batch,),
        in_specs=[
            second((shards, batch, chunks, rows, DELAYS)), lead((batch, DELAYS, DELAYS)),
        ],
        out_specs=[second((1, batch, rows, DELAYS))] * chunks,
        out_shape=[jax.ShapeDtypeStruct((1, items, rows, DELAYS), bf16)] * chunks,
        compiler_params=pltpu.CompilerParams(vmem_limit_bytes=BIG),
    )(received, inverse)
    basis_local_t = basis_local.T
    tall = size + 16

    def clean(h, gathered):
        return pl.pallas_call(
            clean_kernel,
            grid_spec=pltpu.PrefetchScalarGridSpec(
                num_scalar_prefetch=1,
                grid=(items // batch,),
                in_specs=[
                    pl.BlockSpec((batch, size, chan), lambda i, ids: (i, h, 0)),
                    pl.BlockSpec((1, shards, batch, rows, DELAYS), lambda i, ids: (0, 0, i, 0, 0)),
                    full((DELAYS, chan)),
                    lead((batch, 1, chan)),
                ],
                out_specs=full((groups, tall, chan)),
                scratch_shapes=[pltpu.VMEM((groups, tall, chan), f32)],
            ),
            out_shape=jax.ShapeDtypeStruct((groups, tall, chan), bf16),
            compiler_params=pltpu.CompilerParams(vmem_limit_bytes=58 * 1024 * 1024),
            cost_estimate=pl.CostEstimate(
                flops=2_000_000_000, bytes_accessed=4 * items * size * chan, transcendentals=0
            ),
        )(group_id, fringe, gathered, basis_local_t, weight_rows)

    pieces = []
    for h in range(chunks):
        part = coefficients[h]
        if h:
            part, sums = lax.optimization_barrier((part, sums))
        sums = clean(h, gather_chain(part, shards, 1, h))
        if h:
            sums, pieces[-1] = lax.optimization_barrier((sums, pieces[-1]))
        arrived = lax.all_to_all(sums, "bl", split_axis=0, concat_axis=0, tiled=True)
        total = jnp.sum(arrived.reshape(owners, GPO, tall, chan).astype(f32), 0)
        counts = jnp.maximum(total[:, size:size + 1, :1], 1.0)
        mean = (total[:, :size] / counts).astype(bf16).reshape(GPO, shards, rows, chan)
        pieces.append(jnp.transpose(mean, (1, 0, 2, 3)))
    if shards > 8:
        swapped = [
            lax.all_to_all(piece, "freq", split_axis=0, concat_axis=0, tiled=True)
            for piece in pieces
        ]
        swapped = [jnp.concatenate(list(piece), axis=-1) for piece in swapped]
    else:
        me = lax.axis_index("freq")
        swapped = []
        for piece in pieces:
            parts = [lax.dynamic_index_in_dim(piece, me, 0, keepdims=False)]
            for j in range(1, shards):
                out = lax.dynamic_index_in_dim(piece, (me + shards - j) % shards, 0, keepdims=False)
                parts.append(
                    lax.ppermute(out, "freq", [(d, (d - j) % shards) for d in range(shards)])
                )
            doubled = jnp.concatenate(parts + parts, axis=-1)
            offset = (shards - me) % shards * chan
            swapped.append(lax.dynamic_slice_in_dim(doubled, offset, CH, 2))
    averaged = [piece.reshape(GPO, 2 // chunks, time_local, CH) for piece in swapped]
    return jnp.concatenate(averaged, 1)


MESH = pl.DeviceIdType.MESH
RANK = 48


def filter_tables(length, shards):
    sample_index = np.arange(length)
    phase_index = sample_index[:, None] * sample_index[None, :] % length
    angles = phase_index.astype(np.float32) * np.float32(2.0 * math.pi / length)
    cosine = np.cos(angles).astype(jnp.bfloat16).astype(np.float64)
    sine = np.sin(angles).astype(jnp.bfloat16).astype(np.float64)
    signed = (sample_index - length * (sample_index >= length // 2)).astype(np.float64)
    tables = []
    for band in range(NBAND):
        center = (band - (NBAND - 1) / 2.0) * (length / (4.0 * NBAND))
        ratio = (signed - center) / (length / 32.0)
        response = (0.15 + 0.85 / (1.0 + ratio**4)) / length
        even = (cosine * response) @ cosine + (sine * response) @ sine
        odd = (cosine * response) @ sine - (sine * response) @ cosine
        whole = np.concatenate(
            [np.concatenate([even, odd], 1), np.concatenate([-odd, even], 1)], 0
        )
        tables.append(whole)
    tables = np.stack(tables).reshape(NBAND, 2 * length, 2, shards, length // shards)
    tables = np.transpose(tables, (3, 0, 1, 2, 4))
    return tables.reshape(shards, NBAND, 2 * length, 2 * length // shards).astype(jnp.bfloat16)


def factored_basis(channels, modes, shards):
    size = channels // shards
    channel_index = np.arange(channels)
    order_index = np.arange(modes)
    phase = (order_index[None, :] * (2 * channel_index[:, None] + 1) % (4 * channels)).astype(
        np.longdouble
    )
    exact = np.cos(phase * (np.longdouble(np.pi) / (2 * channels)))
    fronts, backs = [], []
    for z in range(shards):
        block = exact[z * size:(z + 1) * size]
        rest = block.copy()
        columns = []
        for _ in range(RANK):
            norms = (rest * rest).sum(0)
            best = int(np.argmax(norms))
            column = rest[:, best] / np.sqrt(norms[best])
            for other in columns:
                column = column - other * (other * column).sum()
            column = column / np.sqrt((column * column).sum())
            columns.append(column)
            rest = rest - column[:, None] * (column[:, None] * rest).sum(0)[None]
        front = np.stack(columns)
        fronts.append(front)
        backs.append(np.stack([(row[:, None] * block).sum(0) for row in front]))
    fronts = np.stack(fronts).astype(np.float32)
    spread = np.zeros((shards, 2, RANK, size, 2), np.float32)
    for r in range(2):
        spread[:, r, :, :, r] = fronts
    fronts = spread.reshape(shards, 2 * RANK, 2 * size).astype(jnp.bfloat16)
    backs = np.concatenate(backs).astype(np.float32).astype(jnp.bfloat16)
    return fronts, backs.T.copy()


def dot_nt(left, right):
    return lax.dot_general(left, right, NT, preferred_element_type=jnp.float32)


def main_kernel(ridge, scales, start_scale, ids, bands, vis_hbm, flags_ref, m_hbm, front_hbm,
                back_ref, basis_hbm, basis_t_hbm, out_ref,
                vis_v, m_v, front_v, basis_v, basis_t_v, sep_a, sep_b, pick_a, pick_b, weight_v, half_v, spread_v, turned_v, sums_a, sums_b,
                pair_send_a, pair_send_b, pair_recv_a, pair_recv_b, cross_send_a, cross_send_b,
                cross_recv_a, cross_recv_b, far_send_a, far_send_b, far_recv_a, far_recv_b,
                y_send, y_recv, w_recv, wide, inv_v, coef_v, coef_send, coef_recv,
                code_tmp, code_send, code_recv, left_v, right_v, fit_v,
                prev_s, last_s, next_s, slot_s, local_sem, send_sem, recv_sem):
    f32, bf16 = jnp.float32, jnp.bfloat16
    items, chan = vis_v.shape[0], vis_v.shape[1]
    length = vis_v.shape[3]
    rt = m_v.shape[3]
    modes = basis_v.shape[1]
    me_b, me_f = lax.axis_index("bl"), lax.axis_index("freq")
    me_x, me_c = me_b // 2, lax.rem(me_b, 2)
    far = [lax.rem(me_f + 2, 4), 3 - me_f, me_f + 1 - 2 * lax.rem(me_f, 2), me_f]
    sibling = me_b + 1 - 2 * me_c
    across = lax.rem(me_b + 2, 4)
    diagonal = 3 - me_b
    owners = [me_b, sibling, across, diagonal]
    sums = (sums_a, sums_b)
    pair_send, pair_recv = (pair_send_a, pair_send_b), (pair_recv_a, pair_recv_b)
    cross_send, cross_recv = (cross_send_a, cross_send_b), (cross_recv_a, cross_recv_b)
    far_send, far_recv = (far_send_a, far_send_b), (far_recv_a, far_recv_b)
    spans = [(0, sums_a.shape[1]), (sums_a.shape[1], sums_b.shape[1])]
    chunk = items // 4

    def load(i):
        return pltpu.make_async_copy(
            vis_hbm.at[pl.ds(i * chunk, chunk)], vis_v.at[pl.ds(i * chunk, chunk)],
            local_sem.at[i],
        )

    tables = [
        pltpu.make_async_copy(m_hbm.at[far[j]], m_v.at[j], local_sem.at[4 + j])
        for j in range(4)
    ]
    bases = [
        pltpu.make_async_copy(basis_hbm, basis_v, local_sem.at[8]),
        pltpu.make_async_copy(basis_t_hbm, basis_t_v, local_sem.at[9]),
    ]
    front = pltpu.make_async_copy(front_hbm.at[me_f], front_v, local_sem.at[10])
    for copy in [load(0), front] + tables + [load(i) for i in range(1, 4)]:
        copy.start()

    barrier = pltpu.get_barrier_semaphore()
    for j in range(3):
        pl.semaphore_signal(barrier, inc=1, device_id={"freq": far[j]}, device_id_type=MESH)
        pl.semaphore_signal(barrier, inc=1, device_id={"bl": owners[j + 1]}, device_id_type=MESH)

    weight_v[...] = 1.0 - flags_ref[...].astype(f32)
    half_v[...] = weight_v[...].astype(bf16)
    repeat = (
        lax.broadcasted_iota(jnp.int32, (chan, 2 * chan), 1) // 2
        == lax.broadcasted_iota(jnp.int32, (chan, 2 * chan), 0)
    ).astype(f32)
    spread_v[...] = dot32(half_v[...], repeat.astype(bf16))
    padded = jnp.concatenate([weight_v[...], jnp.zeros((128 - items, chan), f32)], 0)
    turned_v[...] = padded.T.astype(bf16)
    for total in sums:
        total[0] = jnp.zeros_like(total[0])
    group = [ids[b] for b in range(items)]
    for b in range(items):
        before, after = jnp.int32(0), jnp.int32(items)
        for other in range(b):
            before = jnp.where(group[other] == group[b], other + 1, before)
        for other in reversed(range(b + 1, items)):
            after = jnp.where(group[other] // GPO == group[b] // GPO, other, after)
        prev_s[b] = before
        next_s[b] = after
    next_s[items] = jnp.int32(items)
    for g in range(4 * GPO):
        end = jnp.int32(0)
        for b in range(items):
            end = jnp.where(group[b] == g, b + 1, end)
        last_s[g] = end
    for o in range(4):
        place = jnp.int32(items)
        for b in reversed(range(items)):
            place = jnp.where(group[b] // GPO == o, b, place)
        for step in range(CAP):
            slot_s[o * CAP + step] = place
            place = next_s[place]

    pl.semaphore_wait(barrier, 6)

    pending = []

    def remote(index, source, target, axis, place):
        return pltpu.make_async_remote_copy(
            src_ref=source, dst_ref=target, send_sem=send_sem.at[index],
            recv_sem=recv_sem.at[index], device_id={axis: place}, device_id_type=MESH,
        )

    def send(index, source, target, axis, place):
        copy = remote(index, source, target, axis, place)
        copy.start()
        pending.append(copy)
        return copy

    def y_copy(j, c):
        part = pl.ds(c * chunk, chunk)
        return remote(
            31 + 4 * j + c, y_send.at[j, part], y_recv.at[me_f, part], "freq", far[j]
        )

    w_copies = [send(j, half_v, w_recv.at[me_f], "freq", far[j]) for j in range(3)]

    def separate(b, span, target, pick):
        at, size = span
        values = vis_v[b, at:at + size].astype(f32).reshape(2 * size, length)
        for h in range(length // 128):
            pick[h, :2 * size] = values[:, h * 128:(h + 1) * 128]
        chosen = (lax.broadcasted_iota(jnp.int32, (128, 128), 0) == b).astype(f32).astype(bf16)
        mask = dot32(turned_v[at:at + size], chosen)
        for r in range(2):
            for h in range(length // 128):
                place = r * length + h * 128
                target[:size, place:place + 128] = (
                    pick[h, pl.ds(r, size, stride=2), :] * mask
                ).astype(bf16)

    def table_of(b):
        return jnp.concatenate([m_v[j, bands[b]] for j in range(4)], 1)

    def project(b, target, at):
        rows = vis_v[b].reshape(2 * chan, length)
        picked = front_v[...] * spread_v[pl.ds(b, 1), :].astype(bf16)
        raw = dot32(picked, rows).astype(bf16)
        target[at:at + RANK, :length] = raw[:RANK]
        target[at:at + RANK, length:] = raw[RANK:]

    def filter_one(b, q, source):
        size = spans[q][1]
        rows = size + RANK if q == 0 else size
        fringe = dot32(source[:rows], table_of(b))
        sums[q][b + 1] = sums[q][prev_s[b]] + fringe[:size]
        if q == 0:
            y = fringe[size:].astype(bf16)
            for j in range(3):
                y_send[j, b] = y[:, j * rt:(j + 1) * rt]
            y_recv[me_f, b] = y[:, 3 * rt:]

    for table in tables:
        table.wait()
    front.wait()

    def project_chunk(c, carry):
        load(c).wait()
        for i in range(chunk):
            target, pick = ((sep_a, pick_a), (sep_b, pick_b))[i % 2]
            separate(c * chunk + i, spans[0], target, pick)
            project(c * chunk + i, target, spans[0][1])
            filter_one(c * chunk + i, 0, target)
        for j in range(3):
            y_copy(j, c).start()
        return carry

    lax.fori_loop(0, 4, project_chunk, 0)
    for copy in bases:
        copy.start()

    pair_copies, cross_copies, far_copies = [[], []], [[], []], []

    def filter_span(q, first, last):
        def filter_pair(t, carry):
            separate(2 * t + 1, spans[q], sep_b, pick_b)
            filter_one(2 * t, q, sep_a)
            separate(jnp.minimum(2 * t + 2, items - 1), spans[q], sep_a, pick_a)
            filter_one(2 * t + 1, q, sep_b)
            return carry

        lax.fori_loop(first, last, filter_pair, 0)

    def pair_start(q):
        for j in range(4):
            for x in range(2):
                for l in range(GPO):
                    g = GPO * (2 * x + 1 - me_c) + l
                    part = sums[q][last_s[g], :, j * rt:(j + 1) * rt]
                    pair_send[q][j, GPO * x + l] = part.astype(bf16)
            pair_copies[q].append(
                send(3 + 4 * q + j, pair_send[q].at[j], pair_recv[q].at[j], "bl", sibling)
            )

    def pair_stage(q):
        for j in range(4):
            pair_copies[q][j].wait_recv()
            for l in range(GPO):
                mine = sums[q][last_s[GPO * across + l], :, j * rt:(j + 1) * rt]
                other = pair_recv[q][j, GPO * (1 - me_x) + l].astype(f32)
                cross_send[q][j, l] = (mine + other).astype(bf16)
            cross_copies[q].append(
                send(11 + 4 * q + j, cross_send[q].at[j], cross_recv[q].at[j], "bl", across)
            )

    def cross_stage(q, j):
        cross_copies[q][j].wait_recv()
        for l in range(GPO):
            total = sums[q][last_s[GPO * me_b + l], :, j * rt:(j + 1) * rt]
            total = total + pair_recv[q][j, GPO * me_x + l].astype(f32)
            total = (total + cross_recv[q][j, l].astype(f32)).astype(bf16)
            if j < 3:
                far_send[q][j, l] = total
            else:
                far_recv[q][me_f, l] = total
        if j < 3:
            far_copies.append(
                send(19 + 3 * q + j, far_send[q].at[j], far_recv[q].at[me_f], "freq", far[j])
            )

    pair_start(0)
    separate(0, spans[1], sep_a, pick_a)
    filter_span(1, 0, 2)
    pair_stage(0)
    filter_span(1, 2, items // 2)
    pair_start(1)

    for copy in w_copies:
        copy.wait_recv()
    w_recv[me_f] = half_v[...]
    for z in range(4):
        wide[:items, z * chan:(z + 1) * chan] = w_recv[z].astype(f32)
    wide[items:, :] = jnp.zeros_like(wide[items:, :])

    half = wide.shape[1] // 2
    code_copies = []
    for k in range(4):
        for s in range(CAP):
            place = slot_s[owners[k] * CAP + s]
            local = lax.rem(ids[jnp.minimum(place, items - 1)], GPO) + 1
            code = jnp.where(place < items, local, 0).astype(f32)
            row = wide[pl.ds(place, 1), :] * code
            for h in range(2):
                code_tmp[h * CAP + s:h * CAP + s + 1, :half] = row[:, h * half:(h + 1) * half]
                code_tmp[h * CAP + s:h * CAP + s + 1, half:] = (
                    jnp.zeros((1, code_tmp.shape[1] - half), f32) + code
                )
        if k == 0:
            code_recv[me_b] = code_tmp[...].astype(bf16)
        else:
            code_send[k - 1] = code_tmp[...].astype(bf16)
            code_copies.append(
                send(24 + k, code_send.at[k - 1], code_recv.at[me_b], "bl", owners[k])
            )

    for copy in bases:
        copy.wait()
    eye = (
        lax.broadcasted_iota(jnp.int32, (modes, modes), 0)
        == lax.broadcasted_iota(jnp.int32, (modes, modes), 1)
    ).astype(f32)
    batch = 8

    def invert(step, carry):
        normals = []
        for i in range(batch):
            weight = wide[pl.ds(step * batch + i, 1), :].astype(bf16)
            normals.append(dot32(basis_t_v[...] * weight, basis_v[...]) + ridge * eye)
        guess = [
            scales[0] * (2.0 * start_scale * eye - start_scale * start_scale * normal)
            for normal in normals
        ]
        normals = [halves(normal) for normal in normals]
        for turn, scale in enumerate(scales[1:]):
            parts = [halves(value) for value in guess]
            if turn + 3 < len(scales) - 1:
                product = [dot32(n[0], g[0]) for n, g in zip(normals, parts)]
            else:
                product = [dot_split(n, g) for n, g in zip(normals, parts)]
            error = [(eye - value).astype(bf16) for value in product]
            guess = [
                scale * (value + dot32(g[0], e)) for value, g, e in zip(guess, parts, error)
            ]
        for i in range(batch):
            inv_v[step * batch + i] = guess[i]
        return carry

    cross_stage(0, 0)
    cross_stage(0, 1)
    cross_stage(0, 2)
    cross_stage(0, 3)
    pair_stage(1)
    lax.fori_loop(0, 1, invert, 0)
    lax.fori_loop(1, 2, invert, 0)
    cross_stage(1, 0)

    def solve(p, carry):
        values = y_recv[:, p].reshape(-1, rt)
        projected = dot32(back_ref[...], values).T
        coef_v[p] = dot_split(halves(projected), halves(inv_v[p])).astype(bf16)
        return carry

    for c in range(4):
        for j in range(3):
            y_copy(j, c).wait_recv()
        lax.fori_loop(c * chunk, (c + 1) * chunk, solve, 0, unroll=4)
    coef_v[items] = jnp.zeros_like(coef_v[items])
    coef_copies = []
    for k in (2, 3, 1, 0):
        for s in range(CAP):
            value = coef_v[slot_s[owners[k] * CAP + s]]
            if k == 0:
                coef_recv[me_b, s] = value
            else:
                coef_send[k - 1, s] = value
        if k > 0:
            coef_copies.append(
                send(27 + k, coef_send.at[k - 1], coef_recv.at[me_b], "bl", owners[k])
            )

    cross_stage(1, 1)
    cross_stage(1, 2)
    counts = [jnp.zeros((1, 128), f32) for _ in range(GPO)]
    for k in range(4):
        if k > 0:
            code_copies[k - 1].wait_recv()
        place = owners[k]
        codes = code_recv[place].astype(f32)
        for h in range(2):
            for s in range(CAP):
                row = codes[h * CAP + s:h * CAP + s + 1, :half]
                weight = (row > 0.0).astype(f32).astype(bf16)
                right_v[h, s * modes:(s + 1) * modes, :] = (
                    basis_t_v[:, h * half:(h + 1) * half] * weight
                )
        if k == 3:
            cross_stage(1, 3)
            for copy in far_copies:
                copy.wait_recv()
            for l in range(GPO):
                for z in range(4):
                    for q, (low, size) in enumerate(spans):
                        at = z * chan + low
                        rest = far_recv[q][z, l].astype(f32).T
                        fit_v[l * rt:(l + 1) * rt, at:at + size] = (
                            rest - fit_v[l * rt:(l + 1) * rt, at:at + size]
                        )
        if k > 0:
            coef_copies[{1: 2, 2: 0, 3: 1}[k]].wait_recv()
        for s in range(CAP):
            value = coef_recv[place, s].astype(f32)
            for l in range(GPO):
                match = (codes[s:s + 1, half:half + 128] == 1.0 + l).astype(f32)
                counts[l] = counts[l] + match
                left_v[l * rt:(l + 1) * rt, s * modes:(s + 1) * modes] = (value * match).astype(
                    bf16
                )
        for h in range(2):
            fitted = dot32(left_v[...], right_v[h])
            if k == 0:
                fit_v[:, h * half:(h + 1) * half] = fitted
            elif k == 3:
                for l in range(GPO):
                    share = 1.0 / jnp.maximum(counts[l][:, :1], 1.0)
                    rest = fit_v[l * rt:(l + 1) * rt, h * half:(h + 1) * half]
                    rest = rest - fitted[l * rt:(l + 1) * rt]
                    out_ref[l, :, h * half:(h + 1) * half] = (rest * share).astype(bf16)
            else:
                fit_v[:, h * half:(h + 1) * half] = fit_v[:, h * half:(h + 1) * half] + fitted

    for c in range(4):
        for j in range(3):
            y_copy(j, c).wait_send()
    for copy in pending:
        copy.wait_send()


def per_device_fused(vis, flags, band, group_id):
    items, chan, _, length = vis.shape
    shards = 4
    f32, bf16 = jnp.float32, jnp.bfloat16
    rt = 2 * length // shards
    channels = chan * shards
    smem = pl.BlockSpec(memory_space=pltpu.SMEM)
    vmem = pl.BlockSpec(memory_space=pltpu.VMEM)
    hbm = pl.BlockSpec(memory_space=pltpu.HBM)
    table = jnp.asarray(filter_tables(length, shards))
    fronts, backs = factored_basis(channels, DELAYS, shards)
    basis = make_basis(channels, DELAYS)
    ridge = channels / 64.0
    high = ridge + 1.05 * channels
    half = channels // 2
    narrow = 128
    out = pl.pallas_call(
        functools.partial(main_kernel, ridge, newton_scales(ridge, high), 2.0 / (ridge + high)),
        in_specs=[smem, smem, hbm, vmem, hbm, hbm, vmem, hbm, hbm],
        out_specs=vmem,
        out_shape=jax.ShapeDtypeStruct((GPO, rt, channels), bf16),
        scratch_shapes=[
            pltpu.VMEM(vis.shape, bf16),
            pltpu.VMEM((shards, NBAND, 2 * length, rt), bf16),
            pltpu.VMEM((2 * RANK, 2 * chan), bf16),
            pltpu.VMEM((channels, DELAYS), bf16),
            pltpu.VMEM((DELAYS, channels), bf16),
            pltpu.VMEM((chan, 2 * length), bf16),
            pltpu.VMEM((chan, 2 * length), bf16),
            pltpu.VMEM((length // 128, 2 * chan, 128), f32),
            pltpu.VMEM((length // 128, 2 * chan, 128), f32),
            pltpu.VMEM((items, chan), f32),
            pltpu.VMEM((items, chan), bf16),
            pltpu.VMEM((items, 2 * chan), f32),
            pltpu.VMEM((chan, 128), bf16),
            pltpu.VMEM((items + 1, narrow, 2 * length), f32),
            pltpu.VMEM((items + 1, chan - narrow, 2 * length), f32),
        ] + [
            pltpu.VMEM(lead_shape + (size, rt), bf16)
            for lead_shape in ((4, 2 * GPO), (4, 2 * GPO), (4, GPO), (4, GPO), (3, GPO), (shards, GPO))
            for size in (narrow, chan - narrow)
        ] + [
            pltpu.VMEM((3, items, RANK, rt), bf16),
            pltpu.VMEM((shards, items, RANK, rt), bf16),
            pltpu.VMEM((shards, items, chan), bf16),
            pltpu.VMEM((items + 8, channels), f32),
            pltpu.VMEM((items, DELAYS, DELAYS), f32),
            pltpu.VMEM((items + 1, rt, DELAYS), bf16),
            pltpu.VMEM((3, CAP, rt, DELAYS), bf16),
            pltpu.VMEM((4, CAP, rt, DELAYS), bf16),
            pltpu.VMEM((2 * CAP, half + 128), f32),
            pltpu.VMEM((3, 2 * CAP, half + 128), bf16),
            pltpu.VMEM((4, 2 * CAP, half + 128), bf16),
            pltpu.VMEM((GPO * rt, CAP * DELAYS), bf16),
            pltpu.VMEM((2, CAP * DELAYS, half), bf16),
            pltpu.VMEM((GPO * rt, channels), f32),
            pltpu.SMEM((items,), jnp.int32),
            pltpu.SMEM((4 * GPO,), jnp.int32),
            pltpu.SMEM((items + 1,), jnp.int32),
            pltpu.SMEM((4 * CAP,), jnp.int32),
            pltpu.SemaphoreType.DMA((11,)),
            pltpu.SemaphoreType.DMA((43,)),
            pltpu.SemaphoreType.DMA((43,)),
        ],
        compiler_params=pltpu.CompilerParams(
            collective_id=0, has_side_effects=True, vmem_limit_bytes=56 * 1024 * 1024
        ),
        cost_estimate=pl.CostEstimate(
            flops=10_000_000_000, bytes_accessed=4 * vis.size, transcendentals=0
        ),
    )(
        group_id, band, vis, flags, table, jnp.asarray(fronts), jnp.asarray(backs),
        jnp.asarray(basis), jnp.asarray(basis.T.copy()),
    )
    return out.reshape(GPO, 2, length // shards, channels)


def per_device(vis, flags, band, group_id):
    items, chan, _, length = vis.shape
    fits = (
        lax.axis_size("freq") == 4 and lax.axis_size("bl") == 4 and items == 16
        and chan % 128 == 0 and chan > 128 and length == 256
    )
    return (per_device_fused if fits else per_device_general)(vis, flags, band, group_id)


def solution(mesh):
    in_specs = (P("bl", "freq", None, "win"), P("bl", "freq"), P("bl"), P("bl"))
    out_specs = P("bl", None, ("win", "freq"), None)
    return jax.shard_map(
        per_device, mesh=mesh, in_specs=in_specs, out_specs=out_specs, check_vma=False
    )
```
